32 devices in a mesh: energy: 16 (over z, x, core), mom: 2 (over y).
Axes of the slice: x: 2, y: 2, z: 4, core: 2. Of those that a mesh axis runs over, the one named last changes fastest.
Arguments:
- sigma_in: float32 [64, 2, 2, 256, 256], P('energy', 'mom'), may hold values from -0.1875 to 0.1875
- hamiltonian: float32 [2, 2, 256, 256], P('mom'), may hold values from -0.375 to 0.375
- coupling: float32 [2, 256, 256], P('mom'), may hold values from -0.1875 to 0.1875
- energies: float32 [64], replicated, may hold values from 1.4 to 2, as said below
- counts: int32 [64], replicated, may hold values from 2 to 4, as said below
- strengths: float32 [16], replicated, may hold values from 0.05625 to 0.1875
- offsets: int32 [16], replicated, may hold values from 0 to 1
Outputs:
- sigma_next: float32 [64, 2, 2, 256, 256], P('energy', 'mom')
The draws below stay inside these ranges and needn't reach their ends.
Inputs may be any that keep to these rules, and one draw needn't show every extreme that they name: `energies`: increasing along the grid. `counts`: each point needs either 2 or 4 sweeps, and some point needs 4.
All inputs are finite; a program needn't handle non-finite values.
Results may differ from the reference program's by a relative error of at most 0.0003.
Values sent between devices are 32-bit elements; how exact they have to be, the bound alone decides.
A program may use at most 64 MiB of HBM per device.

```python
import math
import jax
import jax.numpy as jnp
from jax import lax

M = 256
E_DEV = 4
S_LO = 2
S_MAX = 4
NQ = 16
E_TOT = 64
K = 2
N_ENERGY = 16
N_MOM = 2


def draw_energies(key, part):
    key_gaps, key_block = jax.random.split(jax.random.fold_in(key, 3))
    blocks = E_TOT // E_DEV
    wide_gap = min(0.03, 0.24 / E_DEV)
    planted = jax.random.randint(key_block, (), 0, blocks)
    gap_index = jnp.arange(E_TOT - 1, dtype=jnp.int32)
    inside = (gap_index >= planted * E_DEV) & (gap_index < planted * E_DEV + E_DEV - 1)
    raw_gaps = jax.random.uniform(key_gaps, (E_TOT - 1,), jnp.float32, 0.3, 1.0)
    raw_gaps = jnp.where(inside, 0.0, raw_gaps)
    remaining = 0.58 - wide_gap * (E_DEV - 1)
    gaps = jnp.where(inside, wide_gap, raw_gaps * (remaining / jnp.sum(raw_gaps)))
    steps_taken = jnp.concatenate([jnp.zeros((1,), jnp.float32), jnp.cumsum(gaps)])
    return 1.405 + steps_taken


def draw_counts(key, part):
    key_slow, key_place = jax.random.split(jax.random.fold_in(key, 7))
    index = jnp.arange(E_TOT, dtype=jnp.int32)
    low_band = max(E_TOT // 4, 1)
    chance = jnp.where(index < low_band, 10, 1)
    rolled = jax.random.randint(key_slow, (E_TOT,), 0, 20)
    forced = jax.random.randint(key_place, (), 0, low_band)
    slowed = (rolled < chance) | (index == forced)
    return jnp.where(slowed, S_MAX, S_LO).astype(jnp.int32)


def with_ends(drawn, key, smallest, top_value):
    spot = [jax.random.randint(jax.random.fold_in(key, axis), (), 0, length) for axis, length in enumerate(drawn.shape)]
    longest = drawn.shape.index(max(drawn.shape))
    beside = spot[:longest] + [(spot[longest] + 1) % drawn.shape[longest]] + spot[longest + 1:]
    return drawn.at[tuple(spot)].set(smallest).at[tuple(beside)].set(top_value)


def level_of(rng, dims, shards, low, largest):
    gain, own = 1.0, jax.random.fold_in(rng, 6)
    for dim, blocks in shards:
        draws = jnp.exp(jax.random.uniform(jax.random.fold_in(own, dim), (blocks,), jnp.float32, low / len(shards), largest / len(shards)))
        gain = gain * jnp.repeat(draws, dims[dim] // blocks).reshape([-1 if axis == dim else 1 for axis in range(len(dims))])
    return gain


def normal_values(rng, dims, spread, most, shards=(), kind=jnp.bfloat16):
    values = jax.random.normal(rng, dims, jnp.float32) * spread
    if len(shards) > 0:
        values = level_of(rng, dims, shards, -0.22, 0.18) * values
    return jnp.clip(values, min=-most, max=most).astype(kind)


def setup_inputs(seed: int = 0) -> dict:
    seeds = jax.random.split(jax.random.key(seed), 8)
    sigma_in = normal_values(seeds[0], (E_TOT, K, 2, M, M), (4 * M) ** -0.5, 0.1875, ((0, 16), (1, 2)), jnp.float32)
    hamiltonian = normal_values(seeds[1], (K, 2, M, M), M ** -0.5, 0.375, ((0, 2),), jnp.float32)
    coupling = normal_values(seeds[2], (K, M, M), (4 * M) ** -0.5, 0.1875, ((0, 2),), jnp.float32)
    energies = draw_energies(jax.random.fold_in(seeds[7], 71), 0)
    counts = draw_counts(jax.random.fold_in(seeds[7], 71), 0)
    strengths = jnp.clip(jnp.exp(jax.random.uniform(seeds[5], (NQ,), jnp.float32, math.log(0.05625), math.log(0.1875))), 0.05625, 0.1875)
    offsets = with_ends(jax.random.randint(seeds[6], (NQ,), 0, N_MOM), jax.random.fold_in(seeds[6], 1), 0, N_MOM - 1).astype(jnp.int32)
    return dict(sigma_in=sigma_in, hamiltonian=hamiltonian, coupling=coupling, energies=energies, counts=counts, strengths=strengths, offsets=offsets)


PRECISE = lax.Precision.HIGHEST
MIX_RATE = 0.6
PHONON = 0.1
BROADENING = 0.02


def product(left_side, right_side):
    return jnp.dot(left_side, right_side, precision=PRECISE, preferred_element_type=jnp.float32)


def invert(matrix, energy, sweeps):
    identity = jnp.eye(matrix.shape[0], dtype=jnp.float32)
    estimate = identity / energy
    for sweep_index in range(S_MAX):
        updated = 2.0 * estimate - product(estimate, product(matrix, estimate))
        estimate = jnp.where(sweep_index < sweeps, updated, estimate)
    return estimate


def solve_point(ham_block, coupling_block, sigma_pair, energy, sweeps):
    identity = jnp.eye(ham_block.shape[1], dtype=jnp.float32)
    left_matrix = energy * identity - ham_block[0] - sigma_pair[0]
    left_inverse = invert(left_matrix, energy, sweeps)
    inverse_coupled = product(left_inverse, coupling_block)
    coupled_inverse = product(coupling_block.T, left_inverse)
    right_matrix = energy * identity - ham_block[1] - sigma_pair[1] - product(coupling_block.T, inverse_coupled)
    right_green = invert(right_matrix, energy, sweeps)
    left_green = left_inverse + product(product(inverse_coupled, right_green), coupled_inverse)
    return jnp.stack([left_green, right_green])


def lorentz(offset):
    scaled = offset / BROADENING
    return 1.0 / (1.0 + scaled * scaled)


def build_kernel(row_energy, column_energy):
    spacing = row_energy[:, None] - column_energy[None, :]
    kernel = lorentz(spacing - PHONON) + lorentz(spacing + PHONON)
    return kernel / jnp.sum(kernel, axis=1, keepdims=True)


def reference(sigma_in, hamiltonian, coupling, energies, counts, strengths, offsets):
    def per_energy(held_point):
        sigma_row, energy, sweeps = held_point

        def per_momentum(ham_block, coupling_block, sigma_pair):
            return solve_point(ham_block, coupling_block, sigma_pair, energy, sweeps)

        return jax.vmap(per_momentum)(hamiltonian, coupling, sigma_row)

    green_blocks = lax.map(per_energy, (sigma_in, energies, counts))
    shift_index = jnp.arange(K, dtype=jnp.int32)
    weights = jnp.sum(strengths[:, None] * (offsets[:, None] == shift_index[None, :]).astype(jnp.float32), axis=0)
    kernel = build_kernel(energies, energies)
    piece_width = 2 * M * M // N_ENERGY
    flattened = green_blocks.reshape(E_TOT, K, 2 * M * M)

    def per_block(block_index):
        element_block = lax.dynamic_slice_in_dim(flattened, block_index * piece_width, piece_width, 2)
        mixed_sum = weights[0] * element_block
        for offset_step in range(1, K):
            mixed_sum = mixed_sum + weights[offset_step] * jnp.roll(element_block, offset_step, axis=1)
        return jnp.einsum("ae,ekf->akf", kernel, mixed_sum, precision=PRECISE)

    pieces = lax.map(per_block, jnp.arange(N_ENERGY, dtype=jnp.int32))
    sigma_new = jnp.transpose(pieces, (1, 2, 0, 3)).reshape(sigma_in.shape)
    return (1.0 - MIX_RATE) * sigma_in + MIX_RATE * sigma_new
```

```python
import functools

import jax
import jax.numpy as jnp
from jax import lax
from jax.experimental import pallas as pl
from jax.experimental.pallas import tpu as pltpu
from jax.sharding import PartitionSpec as P

PRECISE = lax.Precision.HIGHEST
MIX_RATE = 0.6
PHONON = 0.1
BROADENING = 0.02


def shifted(value, axis, steps):
    count = lax.axis_size(axis)
    pairs = [(source, (source + steps) % count) for source in range(count)]
    return lax.ppermute(value, axis, pairs)


def product(left_side, right_side):
    return jnp.dot(left_side, right_side, precision=PRECISE, preferred_element_type=jnp.float32)


def invert(matrix, energy, sweeps):
    identity = jnp.eye(matrix.shape[0], dtype=jnp.float32)

    def keep_going(carried):
        return carried[0] < sweeps

    def sweep(carried):
        estimate = carried[1]
        return (carried[0] + 1, 2.0 * estimate - product(estimate, product(matrix, estimate)))

    return lax.while_loop(keep_going, sweep, (jnp.int32(0), identity / energy))[1]


def solve_point(ham_block, coupling_block, sigma_pair, energy, sweeps):
    identity = jnp.eye(ham_block.shape[1], dtype=jnp.float32)
    left_matrix = energy * identity - ham_block[0] - sigma_pair[0]
    left_inverse = invert(left_matrix, energy, sweeps)
    inverse_coupled = product(left_inverse, coupling_block)
    coupled_inverse = product(coupling_block.T, left_inverse)
    right_matrix = (
        energy * identity
        - ham_block[1]
        - sigma_pair[1]
        - product(coupling_block.T, inverse_coupled)
    )
    right_green = invert(right_matrix, energy, sweeps)
    left_green = left_inverse + product(product(inverse_coupled, right_green), coupled_inverse)
    return jnp.stack([left_green, right_green])


def lorentz(offset):
    scaled = offset / BROADENING
    return 1.0 / (1.0 + scaled * scaled)


def build_kernel(row_energy, column_energy):
    spacing = row_energy[:, None] - column_energy[None, :]
    kernel = lorentz(spacing - PHONON) + lorentz(spacing + PHONON)
    return kernel / jnp.sum(kernel, axis=1, keepdims=True)


def plain_body(sigma_in, hamiltonian, coupling, energies, counts, strengths, offsets):
    points = sigma_in.shape[0]
    order = sigma_in.shape[3]
    ranks = lax.axis_size("energy")
    moments = lax.axis_size("mom")
    my_rank = lax.axis_index("energy")
    own_energy = lax.dynamic_slice_in_dim(energies, my_rank * points, points)
    own_count = lax.dynamic_slice_in_dim(counts, my_rank * points, points)
    blocks = sigma_in[:, 0]

    def solve_held(held_point):
        return solve_point(hamiltonian[0], coupling[0], held_point[0], held_point[1], held_point[2])

    green_blocks = lax.map(solve_held, (blocks, own_energy, own_count))
    shift_index = jnp.arange(moments, dtype=jnp.int32)
    weights = jnp.sum(
        strengths[:, None] * (offsets[:, None] == shift_index[None, :]).astype(jnp.float32), axis=0
    )
    kernel = build_kernel(energies, energies)
    piece_width = 2 * order * order // ranks
    spread = green_blocks.reshape(points, ranks, moments, piece_width // moments)
    column = lax.all_to_all(spread, "energy", split_axis=1, concat_axis=0, tiled=True)[:, 0]
    rows_all = column.shape[0]
    flat_column = column.reshape(rows_all, -1)
    mixed_sum = weights[0] * flat_column
    for offset_step in range(1, moments):
        mixed_sum = mixed_sum + weights[offset_step] * shifted(flat_column, "mom", offset_step)
    sigma_part = product(kernel, mixed_sum).reshape(column.shape)
    result = lax.all_to_all(sigma_part[:, None], "energy", split_axis=0, concat_axis=1, tiled=True)
    sigma_new = result.reshape(sigma_in.shape)
    return (1.0 - MIX_RATE) * sigma_in + MIX_RATE * sigma_new


SUBLANES = 8
MESH_ID = pl.DeviceIdType.MESH


def split(value):
    high = value.astype(jnp.bfloat16)
    return high, (value - high.astype(jnp.float32)).astype(jnp.bfloat16)


def left_parts(value):
    high, low = split(value)
    return jnp.concatenate([high, low, high], axis=1)


def right_parts(value):
    high, low = split(value)
    return jnp.concatenate([high, high, low], axis=0)


def multiply(left_side, right_side):
    return jnp.dot(left_side, right_side, preferred_element_type=jnp.float32)


def series(ratios, energies, counts, identity):
    order = identity.shape[0]
    squares = [multiply(left_parts(r), right_parts(r)) for r in ratios]
    totals = [identity + r for r in ratios]
    for sweep in (1, 2, 3):
        rights = [right_parts(s) for s in squares]
        if sweep < 3:
            both = [
                multiply(jnp.concatenate([left_parts(t), left_parts(s)], axis=0), q)
                for t, s, q in zip(totals, squares, rights)
            ]
            added = [b[:order] for b in both]
            squares = [b[order:] for b in both]
        else:
            added = [multiply(left_parts(t), q) for t, q in zip(totals, rights)]
        totals = [jnp.where(sweep < c, t + a, t) for t, a, c in zip(totals, added, counts)]
    return [t * (1.0 / e) for t, e in zip(totals, energies)]


def kernel(
    ranks, moments, points, order, held,
    energy_hbm, count_hbm, strength_hbm, offset_hbm, sigma_hbm, ham_hbm, coupling_hbm,
    out_ref,
    green, gathered, mixed_out, wide, across, across_t,
    sigma_ref, ham_ref, coupling_ref, energy_ref, count_ref, strength_ref, offset_ref,
    ready, read_sigma, read_other, send_first, recv_first, send_second, recv_second,
):
    devices = ranks * moments
    side = devices // 2
    group = side // 2
    total = ranks * points
    early = held // 2
    cuts = 2 if order % 256 == 0 else 1
    width = order // cuts
    my_rank = lax.axis_index("energy")
    my_moment = lax.axis_index("mom")
    me = my_rank * moments + my_moment
    my_side = me // side
    spot = lax.rem(me, side)
    near_side = my_side * side
    far_side = (1 - my_side) * side

    def place_of(other):
        return {"energy": other // moments, "mom": lax.rem(other, moments)}

    sources = [
        (ham_hbm, ham_ref), (energy_hbm, energy_ref), (count_hbm, count_ref),
        (coupling_hbm, coupling_ref), (strength_hbm, strength_ref), (offset_hbm, offset_ref),
    ]
    reads = [pltpu.make_async_copy(a, b, read_other.at[n]) for n, (a, b) in enumerate(sources)]
    sigma_reads = [
        pltpu.make_async_copy(sigma_hbm.at[point], sigma_ref.at[point], read_sigma.at[point])
        for point in range(points)
    ]
    for read in [reads[0], sigma_reads[0]] + reads[1:4]:
        read.start()
    barrier = pltpu.get_barrier_semaphore()

    def greet(index, carried):
        other = far_side + lax.rem(spot + index, side)
        pl.semaphore_signal(barrier, inc=1, device_id=place_of(other), device_id_type=MESH_ID)
        return carried

    lax.fori_loop(0, side, greet, 0)
    for read in sigma_reads[1:] + reads[4:]:
        read.start()

    row_index = lax.broadcasted_iota(jnp.int32, (order, order), 0)
    identity = (row_index == lax.broadcasted_iota(jnp.int32, (order, order), 1)).astype(jnp.float32)

    def tile_of(other, piece):
        return (held - 1 - piece) * devices + other

    def send_over(send):
        def over(index, carried):
            turn = lax.div(index, group)
            half = turn * (1 - my_side) + (1 - turn) * my_side
            half = 1 - half
            send(far_side + half * group + lax.rem(spot + index, group))
            return carried

        lax.fori_loop(0, side, over, 0)

    def send_within(send):
        def within(index, carried):
            send(near_side + lax.rem(spot + index, side))
            return carried

        lax.fori_loop(1, side, within, 0)

    def first_of(point, piece, cut):
        semaphore = recv_first.at[piece if piece < early else early + (piece - early) * cuts + cut]
        chosen = slice(None) if piece < early else pl.ds(cut * width, width)
        if piece < early:
            landing = gathered.at[my_moment, piece, my_rank * points + point]
            source_of = lambda other: green.at[point, tile_of(other, piece)]
        else:
            landing = gathered.at[my_moment, piece, pl.ds(my_rank * points, points), :, chosen]
            source_of = lambda other: green.at[:, tile_of(other, piece), :, chosen]

        def send(other):
            pltpu.make_async_remote_copy(
                src_ref=source_of(other), dst_ref=landing,
                send_sem=send_first, recv_sem=semaphore,
                device_id=place_of(other), device_id_type=MESH_ID,
            ).start()

        def keep():
            pltpu.make_async_copy(source_of(me), landing, semaphore).start()

        return send, keep

    for read in reads[:3]:
        read.wait()
    tiles = order // SUBLANES

    def solve(point, carried):
        pltpu.make_async_copy(sigma_hbm.at[point], sigma_ref.at[point], read_sigma.at[point]).wait()
        energy = energy_ref[my_rank * points + point]
        count = count_ref[my_rank * points + point]
        ratio = (ham_ref[0] + sigma_ref[point, 0]) * (1.0 / energy)
        left_inverse = series([ratio], [energy], [count], identity)[0]

        @pl.when(point == 0)
        def _():
            reads[3].wait()
            across[...] = right_parts(coupling_ref[...])
            across_t[...] = left_parts(coupling_ref[...].T)

        coupled = multiply(left_parts(left_inverse), across[...])
        fold = multiply(across_t[...], right_parts(coupled))
        ratio = (ham_ref[1] + sigma_ref[point, 1] + fold) * (1.0 / energy)
        right_green = series([ratio], [energy], [count], identity)[0]
        green[point, tiles:] = right_green.reshape(tiles, SUBLANES, order)

        @pl.when(point == 0)
        def _():
            pl.semaphore_wait(barrier, side)
            mirror = lax.rem(me + side, devices)
            pl.semaphore_signal(ready, inc=1, device_id=place_of(mirror), device_id_type=MESH_ID)

        for piece in range(early):
            send_over(first_of(point, piece, 0)[0])
        back = multiply(across_t[...], right_parts(left_inverse))
        inner = multiply(left_parts(coupled), right_parts(right_green))
        left_green = left_inverse + multiply(left_parts(inner), right_parts(back))
        green[point, :tiles] = left_green.reshape(tiles, SUBLANES, order)

        @pl.when(point == 0)
        def _():
            pl.semaphore_wait(ready, 1)

        for piece in range(early):
            send, keep = first_of(point, piece, 0)
            keep()
            send_within(send)
        return carried

    lax.fori_loop(0, points, solve, 0)

    for piece in range(early, held):
        for cut in range(cuts):
            send, keep = first_of(0, piece, cut)
            keep()
            send_over(send)
            send_within(send)

    for read in reads[4:]:
        read.wait()
    span = total * SUBLANES
    column = lax.broadcasted_iota(jnp.int32, (SUBLANES, span), 1)
    lane_slot = lax.rem(column, SUBLANES)
    lane_point = lax.div(column, SUBLANES)
    same = lane_slot == lax.broadcasted_iota(jnp.int32, (SUBLANES, span), 0)

    def place(index, carried):
        return jnp.where(lane_point == index, energy_ref[index], carried)

    column_energy = lax.fori_loop(0, total, place, jnp.zeros((SUBLANES, span), jnp.float32))

    def build(index, carried):
        spacing = energy_ref[index] - column_energy
        row = lorentz(spacing - PHONON) + lorentz(spacing + PHONON)
        row = jnp.where(same, row, 0.0)
        row = row * (MIX_RATE / jnp.sum(row, axis=1, keepdims=True))
        wide[pl.ds(pl.multiple_of(index * SUBLANES, SUBLANES), SUBLANES), :] = row
        return carried

    lax.fori_loop(0, total, build, 0)
    weights = []
    for step in range(moments):
        weight = jnp.float32(0.0)
        for transfer in range(strength_ref.shape[0]):
            weight = weight + jnp.where(offset_ref[transfer] == step, strength_ref[transfer], 0.0)
        weights.append(weight)

    wide_parts = left_parts(wide[...])
    arrivals = [(piece, 0, slice(None)) for piece in range(early)] + [
        (piece, cut, slice(cut * width, (cut + 1) * width))
        for piece in range(early, held) for cut in range(cuts)
    ]
    for number, (piece, cut, chosen) in enumerate(arrivals):
        arrived = gathered.at[:, piece, :, :, chosen]
        pltpu.make_async_copy(arrived, arrived, recv_first.at[number]).wait()
        for moment in range(moments):
            scattered = weights[0] * gathered[moment, piece, :, :, chosen]
            for step in range(1, moments):
                source = (moment - step) % moments
                scattered = scattered + weights[step] * gathered[source, piece, :, :, chosen]
            columns = scattered.shape[-1]
            result = multiply(wide_parts, right_parts(scattered.reshape(span, columns)))
            mixed_out[moment, piece, :, :, chosen] = result.reshape(total, SUBLANES, columns)

        def give_back(other, piece=piece, chosen=chosen):
            rank = other // moments
            pltpu.make_async_remote_copy(
                src_ref=mixed_out.at[lax.rem(other, moments), piece, pl.ds(rank * points, points), :, chosen],
                dst_ref=out_ref.at[:, tile_of(me, piece), :, chosen],
                send_sem=send_second,
                recv_sem=recv_second,
                device_id=place_of(other),
                device_id_type=MESH_ID,
            ).start()

        send_within(give_back)
        send_over(give_back)
        pltpu.make_async_copy(
            mixed_out.at[my_moment, piece, pl.ds(my_rank * points, points), :, chosen],
            out_ref.at[:, tile_of(me, piece), :, chosen],
            recv_second,
        ).start()

    pltpu.make_async_copy(out_ref, out_ref, recv_second).wait()
    sent = green.at[:, pl.ds(0, (devices - 1) * held)]
    pltpu.make_async_copy(sent, sent, send_first).wait()
    pltpu.make_async_copy(sent, sent, send_second).wait()


def fused_body(sigma_in, hamiltonian, coupling, energies, counts, strengths, offsets):
    points, order = sigma_in.shape[0], sigma_in.shape[3]
    ranks = lax.axis_size("energy")
    moments = lax.axis_size("mom")
    tiles = 2 * order // SUBLANES
    held = tiles // (ranks * moments)
    total = ranks * points
    span = total * SUBLANES
    cuts = 2 if order % 256 == 0 else 1
    hbm = pl.BlockSpec(memory_space=pltpu.HBM)
    operands = (energies, counts, strengths, offsets, sigma_in[:, 0], hamiltonian[0], coupling[0])
    sigma_new = pl.pallas_call(
        functools.partial(kernel, ranks, moments, points, order, held),
        out_shape=jax.ShapeDtypeStruct((points, tiles, SUBLANES, order), jnp.float32),
        in_specs=[hbm] * 7,
        out_specs=pl.BlockSpec(memory_space=pltpu.VMEM),
        scratch_shapes=[
            pltpu.VMEM((points, tiles, SUBLANES, order), jnp.float32),
            pltpu.VMEM((moments, held, total, SUBLANES, order), jnp.float32),
            pltpu.VMEM((moments, held, total, SUBLANES, order), jnp.float32),
            pltpu.VMEM((span, span), jnp.float32),
            pltpu.VMEM((3 * order, order), jnp.bfloat16),
            pltpu.VMEM((order, 3 * order), jnp.bfloat16),
            pltpu.VMEM((points, 2, order, order), jnp.float32),
            pltpu.VMEM((2, order, order), jnp.float32),
            pltpu.VMEM((order, order), jnp.float32),
            pltpu.SMEM(energies.shape, jnp.float32),
            pltpu.SMEM(counts.shape, jnp.int32),
            pltpu.SMEM(strengths.shape, jnp.float32),
            pltpu.SMEM(offsets.shape, jnp.int32),
            pltpu.SemaphoreType.REGULAR,
            pltpu.SemaphoreType.DMA((points,)),
            pltpu.SemaphoreType.DMA((6,)),
            pltpu.SemaphoreType.DMA,
            pltpu.SemaphoreType.DMA((held // 2 * (1 + cuts),)),
            pltpu.SemaphoreType.DMA,
            pltpu.SemaphoreType.DMA,
        ],
        compiler_params=pltpu.CompilerParams(
            collective_id=0, has_side_effects=True, vmem_limit_bytes=32 * 1024 * 1024
        ),
        name="green_and_scatter",
    )(*[pltpu.with_memory_space_constraint(value, pltpu.HBM) for value in operands])
    return (1.0 - MIX_RATE) * sigma_in + sigma_new.reshape(sigma_in.shape)


def body(sigma_in, hamiltonian, coupling, energies, counts, strengths, offsets):
    devices = lax.axis_size("energy") * lax.axis_size("mom")
    tiles = 2 * sigma_in.shape[3] // SUBLANES
    fits = tiles % (2 * devices) == 0 and lax.axis_size("energy") % 4 == 0
    chosen = fused_body if fits else plain_body
    return chosen(sigma_in, hamiltonian, coupling, energies, counts, strengths, offsets)


def solution(mesh):
    placed = (
        P("energy", "mom", None, None, None),
        P("mom", None, None, None),
        P("mom", None, None),
        P(),
        P(),
        P(),
        P(),
    )
    return jax.shard_map(
        body,
        mesh=mesh,
        in_specs=placed,
        out_specs=P("energy", "mom", None, None, None),
        check_vma=False,
    )
```

```python
import functools

import jax
import jax.numpy as jnp
from jax import lax
from jax.experimental import pallas as pl
from jax.experimental.pallas import tpu as pltpu
from jax.sharding import PartitionSpec as P

PRECISE = lax.Precision.HIGHEST
MIX_RATE = 0.6
PHONON = 0.1
BROADENING = 0.02


def shifted(value, axis, steps):
    count = lax.axis_size(axis)
    pairs = [(source, (source + steps) % count) for source in range(count)]
    return lax.ppermute(value, axis, pairs)


def product(left_side, right_side):
    return jnp.dot(left_side, right_side, precision=PRECISE, preferred_element_type=jnp.float32)


def invert(matrix, energy, sweeps):
    identity = jnp.eye(matrix.shape[0], dtype=jnp.float32)

    def keep_going(carried):
        return carried[0] < sweeps

    def sweep(carried):
        estimate = carried[1]
        return (carried[0] + 1, 2.0 * estimate - product(estimate, product(matrix, estimate)))

    return lax.while_loop(keep_going, sweep, (jnp.int32(0), identity / energy))[1]


def solve_point(ham_block, coupling_block, sigma_pair, energy, sweeps):
    identity = jnp.eye(ham_block.shape[1], dtype=jnp.float32)
    left_matrix = energy * identity - ham_block[0] - sigma_pair[0]
    left_inverse = invert(left_matrix, energy, sweeps)
    inverse_coupled = product(left_inverse, coupling_block)
    coupled_inverse = product(coupling_block.T, left_inverse)
    right_matrix = (
        energy * identity
        - ham_block[1]
        - sigma_pair[1]
        - product(coupling_block.T, inverse_coupled)
    )
    right_green = invert(right_matrix, energy, sweeps)
    left_green = left_inverse + product(product(inverse_coupled, right_green), coupled_inverse)
    return jnp.stack([left_green, right_green])


def lorentz(offset):
    scaled = offset / BROADENING
    return 1.0 / (1.0 + scaled * scaled)


def build_kernel(row_energy, column_energy):
    spacing = row_energy[:, None] - column_energy[None, :]
    kernel = lorentz(spacing - PHONON) + lorentz(spacing + PHONON)
    return kernel / jnp.sum(kernel, axis=1, keepdims=True)


def plain_body(sigma_in, hamiltonian, coupling, energies, counts, strengths, offsets):
    points = sigma_in.shape[0]
    order = sigma_in.shape[3]
    ranks = lax.axis_size("energy")
    moments = lax.axis_size("mom")
    my_rank = lax.axis_index("energy")
    own_energy = lax.dynamic_slice_in_dim(energies, my_rank * points, points)
    own_count = lax.dynamic_slice_in_dim(counts, my_rank * points, points)
    blocks = sigma_in[:, 0]

    def solve_held(held_point):
        return solve_point(hamiltonian[0], coupling[0], held_point[0], held_point[1], held_point[2])

    green_blocks = lax.map(solve_held, (blocks, own_energy, own_count))
    shift_index = jnp.arange(moments, dtype=jnp.int32)
    weights = jnp.sum(
        strengths[:, None] * (offsets[:, None] == shift_index[None, :]).astype(jnp.float32), axis=0
    )
    kernel = build_kernel(energies, energies)
    piece_width = 2 * order * order // ranks
    spread = green_blocks.reshape(points, ranks, moments, piece_width // moments)
    column = lax.all_to_all(spread, "energy", split_axis=1, concat_axis=0, tiled=True)[:, 0]
    rows_all = column.shape[0]
    flat_column = column.reshape(rows_all, -1)
    mixed_sum = weights[0] * flat_column
    for offset_step in range(1, moments):
        mixed_sum = mixed_sum + weights[offset_step] * shifted(flat_column, "mom", offset_step)
    sigma_part = product(kernel, mixed_sum).reshape(column.shape)
    result = lax.all_to_all(sigma_part[:, None], "energy", split_axis=0, concat_axis=1, tiled=True)
    sigma_new = result.reshape(sigma_in.shape)
    return (1.0 - MIX_RATE) * sigma_in + MIX_RATE * sigma_new


SUBLANES = 8
MESH_ID = pl.DeviceIdType.MESH


def split(value):
    high = value.astype(jnp.bfloat16)
    return high, (value - high.astype(jnp.float32)).astype(jnp.bfloat16)


def left_parts(value):
    high, low = split(value)
    return jnp.concatenate([high, low, high], axis=1)


def right_parts(value):
    high, low = split(value)
    return jnp.concatenate([high, high, low], axis=0)


def multiply(left_side, right_side):
    return jnp.dot(left_side, right_side, preferred_element_type=jnp.float32)


def series(ratio, energy, count, identity):
    order = identity.shape[0]
    square = multiply(left_parts(ratio), right_parts(ratio))
    total = identity + ratio
    right = right_parts(square)
    both = multiply(jnp.concatenate([left_parts(total), left_parts(square)], axis=0), right)
    short = total + both[:order]
    square = both[order:]
    right = right_parts(square)
    both = multiply(jnp.concatenate([left_parts(short), left_parts(square)], axis=0), right)
    total = short + both[:order]
    square = both[order:]
    total = total + multiply(left_parts(total), right_parts(square))
    return jnp.where(count > 2, total, short) * (1.0 / energy)


def kernel(
    ranks, moments, points, order, held,
    energy_hbm, count_hbm, strength_hbm, offset_hbm, sigma_hbm, ham_hbm, coupling_hbm,
    out_ref, sigma_ref,
    green, gathered, mixed_out, wide, across, across_t,
    ham_ref, coupling_ref, energy_ref, count_ref, strength_ref, offset_ref,
    ready, read_sigma, read_other, send_first, recv_first, send_second, recv_second,
):
    devices = ranks * moments
    side = devices // 2
    group = side // 2
    total = ranks * points
    early = held // 2
    cuts = 2 if order % 256 == 0 else 1
    width = order // cuts
    my_rank = lax.axis_index("energy")
    my_moment = lax.axis_index("mom")
    me = my_rank * moments + my_moment
    my_side = me // side
    spot = lax.rem(me, side)
    near_side = my_side * side
    far_side = (1 - my_side) * side

    def place_of(other):
        return {"energy": other // moments, "mom": lax.rem(other, moments)}

    sources = [
        (coupling_hbm, coupling_ref), (ham_hbm.at[0], ham_ref.at[0]), (ham_hbm.at[1], ham_ref.at[1]),
        (energy_hbm, energy_ref), (count_hbm, count_ref), (strength_hbm, strength_ref), (offset_hbm, offset_ref),
    ]
    reads = [pltpu.make_async_copy(a, b, read_other.at[n]) for n, (a, b) in enumerate(sources)]

    def sigma_read(point, slab):
        return pltpu.make_async_copy(
            sigma_hbm.at[point, slab], sigma_ref.at[point, slab], read_sigma.at[point, slab]
        )

    for read in [reads[0], reads[1], sigma_read(0, 0), reads[3], reads[4], reads[2], sigma_read(0, 1)]:
        read.start()
    barrier = pltpu.get_barrier_semaphore()

    def greet(index, carried):
        other = far_side + lax.rem(spot + index, side)
        pl.semaphore_signal(barrier, inc=1, device_id=place_of(other), device_id_type=MESH_ID)
        return carried

    lax.fori_loop(0, side, greet, 0)
    for read in reads[5:]:
        read.start()

    def read_point(point, carried):
        sigma_read(point, 0).start()
        sigma_read(point, 1).start()
        return carried

    lax.fori_loop(1, points, read_point, 0)

    row_index = lax.broadcasted_iota(jnp.int32, (order, order), 0)
    identity = (row_index == lax.broadcasted_iota(jnp.int32, (order, order), 1)).astype(jnp.float32)

    def tile_of(other, piece):
        return (held - 1 - piece) * devices + other

    quarter = ranks // 4
    blocks = quarter // 2
    my_block = lax.rem(lax.div(my_rank, 2), blocks)
    my_core = lax.rem(my_rank, 2)

    def send_over(send):
        def over(index, carried):
            turn = lax.div(index, group)
            layer = turn * my_side + (1 - turn) * (1 - my_side)
            step = group - 1 - lax.rem(index, group)
            block = lax.rem(my_block + lax.div(step, 2 * moments), blocks)
            moment = lax.rem(my_moment + lax.rem(lax.div(step, 2), moments), moments)
            core = lax.rem(my_core + lax.rem(step, 2), 2)
            rank = (1 - my_side) * (ranks // 2) + layer * quarter + block * 2 + core
            send(rank * moments + moment)
            return carried

        lax.fori_loop(0, side, over, 0)

    def send_within(send):
        def within(index, carried):
            send(near_side + lax.rem(spot + index, side))
            return carried

        lax.fori_loop(1, side, within, 0)

    def first_of(piece, semaphore, point=None, cut=None):
        if cut is None:
            landing = gathered.at[my_moment, piece, my_rank * points + point]
            source_of = lambda other: green.at[point, tile_of(other, piece)]
        else:
            later, chosen = pl.ds(1, points - 1), pl.ds(cut * width, width)
            landing = gathered.at[my_moment, piece, pl.ds(my_rank * points + 1, points - 1), :, chosen]
            source_of = lambda other: green.at[later, tile_of(other, piece), :, chosen]

        def send(other):
            pltpu.make_async_remote_copy(
                src_ref=source_of(other), dst_ref=landing,
                send_sem=send_first, recv_sem=recv_first.at[semaphore],
                device_id=place_of(other), device_id_type=MESH_ID,
            ).start()

        def keep():
            pltpu.make_async_copy(source_of(me), landing, recv_first.at[semaphore]).start()

        return send, keep

    reads[0].wait()
    across[...] = right_parts(coupling_ref[...])
    across_t[...] = left_parts(coupling_ref[...].T)
    reads[3].wait()
    reads[4].wait()
    reads[1].wait()
    reads[2].wait()
    tiles = order // SUBLANES

    def solve(point, carried):
        sigma_read(point, 0).wait()
        energy = energy_ref[my_rank * points + point]
        count = count_ref[my_rank * points + point]
        ratio = (ham_ref[0] + sigma_ref[point, 0]) * (1.0 / energy)
        left_inverse = series(ratio, energy, count, identity)

        coupled = multiply(left_parts(left_inverse), across[...])
        fold = multiply(across_t[...], right_parts(coupled))
        sigma_read(point, 1).wait()
        ratio = (ham_ref[1] + sigma_ref[point, 1] + fold) * (1.0 / energy)
        right_green = series(ratio, energy, count, identity)
        green[point, tiles:] = right_green.reshape(tiles, SUBLANES, order)

        @pl.when(point == 0)
        def _():
            pl.semaphore_wait(barrier, side)
            mirror = lax.rem(me + side, devices)
            pl.semaphore_signal(ready, inc=1, device_id=place_of(mirror), device_id_type=MESH_ID)

        for piece in range(early):
            send_over(first_of(piece, piece, point=point)[0])
        back = multiply(across_t[...], right_parts(left_inverse))
        inner = multiply(left_parts(coupled), right_parts(right_green))
        left_green = left_inverse + multiply(left_parts(inner), right_parts(back))
        green[point, :tiles] = left_green.reshape(tiles, SUBLANES, order)

        @pl.when(point == 0)
        def _():
            pl.semaphore_wait(ready, 1)

        for piece in range(early):
            send, keep = first_of(piece, piece, point=point)
            keep()
            send_within(send)

        @pl.when(point == 0)
        def _():
            for piece in range(early, held):
                send, keep = first_of(piece, piece, point=0)
                keep()
                send_over(send)
                send_within(send)

        return carried

    lax.fori_loop(0, points, solve, 0)

    for piece in range(early, held):
        for cut in range(cuts):
            send, keep = first_of(piece, held + (piece - early) * cuts + cut, cut=cut)
            keep()
            send_over(send)
            send_within(send)

    for read in reads[5:]:
        read.wait()
    span = total * SUBLANES
    column = lax.broadcasted_iota(jnp.int32, (SUBLANES, span), 1)
    lane_slot = lax.rem(column, SUBLANES)
    lane_point = lax.div(column, SUBLANES)
    same = lane_slot == lax.broadcasted_iota(jnp.int32, (SUBLANES, span), 0)

    def place(index, carried):
        return jnp.where(lane_point == index, energy_ref[index], carried)

    column_energy = lax.fori_loop(0, total, place, jnp.zeros((SUBLANES, span), jnp.float32))

    def build(index, carried):
        spacing = energy_ref[index] - column_energy
        row = lorentz(spacing - PHONON) + lorentz(spacing + PHONON)
        row = jnp.where(same, row, 0.0)
        row = row * (MIX_RATE / jnp.sum(row, axis=1, keepdims=True))
        wide[pl.ds(pl.multiple_of(index * SUBLANES, SUBLANES), SUBLANES), :] = row
        return carried

    lax.fori_loop(0, total, build, 0)
    weights = []
    for step in range(moments):
        weight = jnp.float32(0.0)
        for transfer in range(strength_ref.shape[0]):
            weight = weight + jnp.where(offset_ref[transfer] == step, strength_ref[transfer], 0.0)
        weights.append(weight)

    wide_parts = left_parts(wide[...])
    arrivals = [(piece, None) for piece in range(early)] + [
        (piece, cut) for piece in range(early, held) for cut in range(cuts)
    ]

    def settle(landed, semaphore):
        pltpu.make_async_copy(landed, landed, recv_first.at[semaphore]).wait()

    for piece, cut in arrivals:
        if cut is None:
            chosen = slice(None)
            settle(gathered.at[:, piece], piece)
        else:
            chosen = slice(cut * width, (cut + 1) * width)
            if cut == 0:
                settle(gathered.at[:, piece, pl.ds(0, ranks)], piece)
            settle(
                gathered.at[:, piece, pl.ds(0, total - ranks), :, chosen],
                held + (piece - early) * cuts + cut,
            )
        for moment in range(moments):
            scattered = weights[0] * gathered[moment, piece, :, :, chosen]
            for step in range(1, moments):
                source = (moment - step) % moments
                scattered = scattered + weights[step] * gathered[source, piece, :, :, chosen]
            columns = scattered.shape[-1]
            result = multiply(wide_parts, right_parts(scattered.reshape(span, columns)))
            mixed_out[moment, piece, :, :, chosen] = result.reshape(total, SUBLANES, columns)

        def give_back(other, piece=piece, chosen=chosen):
            rank = other // moments
            pltpu.make_async_remote_copy(
                src_ref=mixed_out.at[lax.rem(other, moments), piece, pl.ds(rank * points, points), :, chosen],
                dst_ref=out_ref.at[:, tile_of(me, piece), :, chosen],
                send_sem=send_second,
                recv_sem=recv_second,
                device_id=place_of(other),
                device_id_type=MESH_ID,
            ).start()

        send_over(give_back)
        send_within(give_back)
        pltpu.make_async_copy(
            mixed_out.at[my_moment, piece, pl.ds(my_rank * points, points), :, chosen],
            out_ref.at[:, tile_of(me, piece), :, chosen],
            recv_second,
        ).start()

    pltpu.make_async_copy(out_ref, out_ref, recv_second).wait()
    sent = green.at[:, pl.ds(0, (devices - 1) * held)]
    pltpu.make_async_copy(sent, sent, send_first).wait()
    pltpu.make_async_copy(sent, sent, send_second).wait()


def fused_body(sigma_in, hamiltonian, coupling, energies, counts, strengths, offsets):
    points, order = sigma_in.shape[0], sigma_in.shape[3]
    ranks = lax.axis_size("energy")
    moments = lax.axis_size("mom")
    tiles = 2 * order // SUBLANES
    held = tiles // (ranks * moments)
    total = ranks * points
    span = total * SUBLANES
    cuts = 2 if order % 256 == 0 else 1
    hbm = pl.BlockSpec(memory_space=pltpu.HBM)
    operands = (energies, counts, strengths, offsets, sigma_in[:, 0], hamiltonian[0], coupling[0])
    sigma_new, sigma_held = pl.pallas_call(
        functools.partial(kernel, ranks, moments, points, order, held),
        out_shape=[
            jax.ShapeDtypeStruct((points, tiles, SUBLANES, order), jnp.float32),
            jax.ShapeDtypeStruct((points, 2, order, order), jnp.float32),
        ],
        in_specs=[hbm] * 7,
        out_specs=[pl.BlockSpec(memory_space=pltpu.VMEM)] * 2,
        scratch_shapes=[
            pltpu.VMEM((points, tiles, SUBLANES, order), jnp.float32),
            pltpu.VMEM((moments, held, total, SUBLANES, order), jnp.float32),
            pltpu.VMEM((moments, held, total, SUBLANES, order), jnp.float32),
            pltpu.VMEM((span, span), jnp.float32),
            pltpu.VMEM((3 * order, order), jnp.bfloat16),
            pltpu.VMEM((order, 3 * order), jnp.bfloat16),
            pltpu.VMEM((2, order, order), jnp.float32),
            pltpu.VMEM((order, order), jnp.float32),
            pltpu.SMEM(energies.shape, jnp.float32),
            pltpu.SMEM(counts.shape, jnp.int32),
            pltpu.SMEM(strengths.shape, jnp.float32),
            pltpu.SMEM(offsets.shape, jnp.int32),
            pltpu.SemaphoreType.REGULAR,
            pltpu.SemaphoreType.DMA((points, 2)),
            pltpu.SemaphoreType.DMA((7,)),
            pltpu.SemaphoreType.DMA,
            pltpu.SemaphoreType.DMA((held + held // 2 * cuts,)),
            pltpu.SemaphoreType.DMA,
            pltpu.SemaphoreType.DMA,
        ],
        compiler_params=pltpu.CompilerParams(
            collective_id=0, has_side_effects=True, vmem_limit_bytes=32 * 1024 * 1024
        ),
        name="green_and_scatter",
    )(*[pltpu.with_memory_space_constraint(value, pltpu.HBM) for value in operands])
    result = (1.0 - MIX_RATE) * sigma_held.reshape(sigma_in.shape) + sigma_new.reshape(sigma_in.shape)
    return result


def body(sigma_in, hamiltonian, coupling, energies, counts, strengths, offsets):
    devices = lax.axis_size("energy") * lax.axis_size("mom")
    tiles = 2 * sigma_in.shape[3] // SUBLANES
    fits = tiles % (2 * devices) == 0 and lax.axis_size("energy") % 8 == 0 and sigma_in.shape[0] > 1
    chosen = fused_body if fits else plain_body
    return chosen(sigma_in, hamiltonian, coupling, energies, counts, strengths, offsets)


def solution(mesh):
    placed = (
        P("energy", "mom", None, None, None),
        P("mom", None, None, None),
        P("mom", None, None),
        P(),
        P(),
        P(),
        P(),
    )
    return jax.shard_map(
        body,
        mesh=mesh,
        in_specs=placed,
        out_specs=P("energy", "mom", None, None, None),
        check_vma=False,
    )
```

```python
import functools

import jax
import jax.numpy as jnp
from jax import lax
from jax.experimental import pallas as pl
from jax.experimental.pallas import tpu as pltpu
from jax.sharding import PartitionSpec as P

PRECISE = lax.Precision.HIGHEST
MIX_RATE = 0.6
PHONON = 0.1
BROADENING = 0.02


def shifted(value, axis, steps):
    count = lax.axis_size(axis)
    pairs = [(source, (source + steps) % count) for source in range(count)]
    return lax.ppermute(value, axis, pairs)


def product(left_side, right_side):
    return jnp.dot(left_side, right_side, precision=PRECISE, preferred_element_type=jnp.float32)


def invert(matrix, energy, sweeps):
    identity = jnp.eye(matrix.shape[0], dtype=jnp.float32)

    def keep_going(carried):
        return carried[0] < sweeps

    def sweep(carried):
        estimate = carried[1]
        return (carried[0] + 1, 2.0 * estimate - product(estimate, product(matrix, estimate)))

    return lax.while_loop(keep_going, sweep, (jnp.int32(0), identity / energy))[1]


def solve_point(ham_block, coupling_block, sigma_pair, energy, sweeps):
    identity = jnp.eye(ham_block.shape[1], dtype=jnp.float32)
    left_matrix = energy * identity - ham_block[0] - sigma_pair[0]
    left_inverse = invert(left_matrix, energy, sweeps)
    inverse_coupled = product(left_inverse, coupling_block)
    coupled_inverse = product(coupling_block.T, left_inverse)
    right_matrix = (
        energy * identity
        - ham_block[1]
        - sigma_pair[1]
        - product(coupling_block.T, inverse_coupled)
    )
    right_green = invert(right_matrix, energy, sweeps)
    left_green = left_inverse + product(product(inverse_coupled, right_green), coupled_inverse)
    return jnp.stack([left_green, right_green])


def lorentz(offset):
    scaled = offset / BROADENING
    return 1.0 / (1.0 + scaled * scaled)


def build_kernel(row_energy, column_energy):
    spacing = row_energy[:, None] - column_energy[None, :]
    kernel = lorentz(spacing - PHONON) + lorentz(spacing + PHONON)
    return kernel / jnp.sum(kernel, axis=1, keepdims=True)


def plain_body(sigma_in, hamiltonian, coupling, energies, counts, strengths, offsets):
    points = sigma_in.shape[0]
    order = sigma_in.shape[3]
    ranks = lax.axis_size("energy")
    moments = lax.axis_size("mom")
    my_rank = lax.axis_index("energy")
    own_energy = lax.dynamic_slice_in_dim(energies, my_rank * points, points)
    own_count = lax.dynamic_slice_in_dim(counts, my_rank * points, points)
    blocks = sigma_in[:, 0]

    def solve_held(held_point):
        return solve_point(hamiltonian[0], coupling[0], held_point[0], held_point[1], held_point[2])

    green_blocks = lax.map(solve_held, (blocks, own_energy, own_count))
    shift_index = jnp.arange(moments, dtype=jnp.int32)
    weights = jnp.sum(
        strengths[:, None] * (offsets[:, None] == shift_index[None, :]).astype(jnp.float32), axis=0
    )
    kernel = build_kernel(energies, energies)
    piece_width = 2 * order * order // ranks
    spread = green_blocks.reshape(points, ranks, moments, piece_width // moments)
    column = lax.all_to_all(spread, "energy", split_axis=1, concat_axis=0, tiled=True)[:, 0]
    rows_all = column.shape[0]
    flat_column = column.reshape(rows_all, -1)
    mixed_sum = weights[0] * flat_column
    for offset_step in range(1, moments):
        mixed_sum = mixed_sum + weights[offset_step] * shifted(flat_column, "mom", offset_step)
    sigma_part = product(kernel, mixed_sum).reshape(column.shape)
    result = lax.all_to_all(sigma_part[:, None], "energy", split_axis=0, concat_axis=1, tiled=True)
    sigma_new = result.reshape(sigma_in.shape)
    return (1.0 - MIX_RATE) * sigma_in + MIX_RATE * sigma_new


SUBLANES = 8
MESH_ID = pl.DeviceIdType.MESH


def split(value):
    high = value.astype(jnp.bfloat16)
    return high, (value - high.astype(jnp.float32)).astype(jnp.bfloat16)


left_parts = right_parts = split


def multiply(left_side, right_side):
    (high, low), (near, far) = left_side, right_side
    rows = high.shape[0] // 2
    both = [
        jnp.dot(jnp.concatenate([high[n * rows:(n + 1) * rows], low[n * rows:(n + 1) * rows]], axis=0), near, preferred_element_type=jnp.float32)
        for n in range(2)
    ]
    last = [jnp.dot(high[n * rows:(n + 1) * rows], far, preferred_element_type=jnp.float32) for n in range(2)]
    return jnp.concatenate([b[:rows] + b[rows:] + l for b, l in zip(both, last)], axis=0)


def series(ratio, energy, count, identity):
    square = multiply(left_parts(ratio), right_parts(ratio))
    total = identity + ratio
    right = right_parts(square)
    fourth = multiply(left_parts(square), right)
    short = total + multiply(left_parts(total), right)
    right = right_parts(fourth)
    eighth = multiply(left_parts(fourth), right)
    total = short + multiply(left_parts(short), right)
    total = total + multiply(left_parts(total), right_parts(eighth))
    return jnp.where(count > 2, total, short) * (1.0 / energy)


def powers(ratio, count, identity):
    square = multiply(left_parts(ratio), right_parts(ratio))
    total = identity + ratio
    right = right_parts(square)
    fourth = multiply(left_parts(square), right)
    short = total + multiply(left_parts(total), right)
    fourth = jnp.where(count > 2, fourth, 0.0)
    right = right_parts(fourth)
    eighth = multiply(left_parts(fourth), right)
    total = short + multiply(left_parts(short), right)
    return total, eighth


def kernel(
    ranks, moments, points, order, held,
    energy_hbm, count_hbm, strength_hbm, offset_hbm, sigma_hbm, ham_hbm, coupling_hbm,
    out_ref, sigma_ref,
    green, gathered, mixed_out, wide, across, across_t,
    ham_ref, coupling_ref, energy_ref, count_ref, strength_ref, offset_ref,
    ready, read_sigma, read_other, send_first, recv_first, send_second, recv_second,
):
    devices = ranks * moments
    side = devices // 2
    group = side // 2
    total = ranks * points
    early = held // 2
    cuts = 2 if order % 256 == 0 else 1
    width = order // cuts
    my_rank = lax.axis_index("energy")
    my_moment = lax.axis_index("mom")
    me = my_rank * moments + my_moment
    my_side = me // side
    spot = lax.rem(me, side)
    near_side = my_side * side
    far_side = (1 - my_side) * side

    def place_of(other):
        return {"energy": other // moments, "mom": lax.rem(other, moments)}

    sources = [
        (coupling_hbm, coupling_ref), (ham_hbm.at[0], ham_ref.at[0]), (ham_hbm.at[1], ham_ref.at[1]),
        (energy_hbm, energy_ref), (count_hbm, count_ref), (strength_hbm, strength_ref), (offset_hbm, offset_ref),
    ]
    reads = [pltpu.make_async_copy(a, b, read_other.at[n]) for n, (a, b) in enumerate(sources)]

    def sigma_read(point, slab):
        return pltpu.make_async_copy(
            sigma_hbm.at[point, slab], sigma_ref.at[point, slab], read_sigma.at[point, slab]
        )

    for read in [reads[0], reads[1], sigma_read(0, 0), reads[3], reads[4], reads[2], sigma_read(0, 1)]:
        read.start()
    barrier = pltpu.get_barrier_semaphore()

    def greet(index, carried):
        other = far_side + lax.rem(spot + index, side)
        pl.semaphore_signal(barrier, inc=1, device_id=place_of(other), device_id_type=MESH_ID)
        return carried

    lax.fori_loop(0, side, greet, 0)
    for read in reads[5:]:
        read.start()

    def read_point(point, carried):
        sigma_read(point, 0).start()
        sigma_read(point, 1).start()
        return carried

    lax.fori_loop(1, points, read_point, 0)

    row_index = lax.broadcasted_iota(jnp.int32, (order, order), 0)
    identity = (row_index == lax.broadcasted_iota(jnp.int32, (order, order), 1)).astype(jnp.float32)

    def tile_of(other, piece):
        return (held - 1 - piece) * devices + other

    quarter = ranks // 4
    blocks = quarter // 2
    my_block = lax.rem(lax.div(my_rank, 2), blocks)
    my_core = lax.rem(my_rank, 2)

    def send_over(send):
        def over(index, carried):
            turn = lax.div(index, group)
            layer = turn * my_side + (1 - turn) * (1 - my_side)
            step = group - 1 - lax.rem(index, group)
            block = lax.rem(my_block + lax.div(step, 2 * moments), blocks)
            moment = lax.rem(my_moment + lax.rem(lax.div(step, 2), moments), moments)
            core = lax.rem(my_core + lax.rem(step, 2), 2)
            rank = (1 - my_side) * (ranks // 2) + layer * quarter + block * 2 + core
            send(rank * moments + moment)
            return carried

        lax.fori_loop(0, side, over, 0)

    def send_within(send):
        def within(index, carried):
            send(near_side + lax.rem(spot + index, side))
            return carried

        lax.fori_loop(1, side, within, 0)

    def first_of(piece, semaphore, point=None, cut=None):
        if cut is None:
            landing = gathered.at[my_moment, piece, my_rank * points + point]
            source_of = lambda other: green.at[point, tile_of(other, piece)]
        else:
            later, chosen = pl.ds(1, points - 1), pl.ds(cut * width, width)
            landing = gathered.at[my_moment, piece, pl.ds(my_rank * points + 1, points - 1), :, chosen]
            source_of = lambda other: green.at[later, tile_of(other, piece), :, chosen]

        def send(other):
            pltpu.make_async_remote_copy(
                src_ref=source_of(other), dst_ref=landing,
                send_sem=send_first, recv_sem=recv_first.at[semaphore],
                device_id=place_of(other), device_id_type=MESH_ID,
            ).start()

        def keep():
            pltpu.make_async_copy(source_of(me), landing, recv_first.at[semaphore]).start()

        return send, keep

    reads[0].wait()
    across[0], across[1] = split(coupling_ref[...])
    across_t[0], across_t[1] = split(coupling_ref[...].T)
    reads[3].wait()
    reads[4].wait()
    reads[1].wait()
    reads[2].wait()
    tiles = order // SUBLANES

    def solve(point, carried):
        sigma_read(point, 0).wait()
        energy = energy_ref[my_rank * points + point]
        count = count_ref[my_rank * points + point]
        ratio = (ham_ref[0] + sigma_ref[point, 0]) * (1.0 / energy)
        total, last = powers(ratio, count, identity)
        spread = coupling_ref[...] + multiply(left_parts(last), (across[0], across[1]))
        back = multiply((across_t[0], across_t[1]), right_parts(total))

        fold = multiply(left_parts(back), right_parts(spread)) * (1.0 / energy)
        sigma_read(point, 1).wait()
        ratio = (ham_ref[1] + sigma_ref[point, 1] + fold) * (1.0 / energy)
        right_green = series(ratio, energy, count, identity)
        green[point, tiles:] = right_green.reshape(tiles, SUBLANES, order)

        @pl.when(point == 0)
        def _():
            pl.semaphore_wait(barrier, side)
            mirror = lax.rem(me + side, devices)
            pl.semaphore_signal(ready, inc=1, device_id=place_of(mirror), device_id_type=MESH_ID)

        for piece in range(early):
            send_over(first_of(piece, piece, point=point)[0])
        right = right_parts(last)
        left_inverse = (total + multiply(left_parts(total), right)) * (1.0 / energy)
        back = (back + multiply(left_parts(back), right)) * (1.0 / energy)
        coupled = multiply(left_parts(total), right_parts(spread)) * (1.0 / energy)
        inner = multiply(left_parts(coupled), right_parts(right_green))
        left_green = left_inverse + multiply(left_parts(inner), right_parts(back))
        green[point, :tiles] = left_green.reshape(tiles, SUBLANES, order)

        @pl.when(point == 0)
        def _():
            pl.semaphore_wait(ready, 1)

        for piece in range(early):
            send, keep = first_of(piece, piece, point=point)
            keep()
            send_within(send)

        @pl.when(point == 0)
        def _():
            for piece in range(early, held):
                send, keep = first_of(piece, piece, point=0)
                keep()
                send_over(send)
                send_within(send)

        return carried

    lax.fori_loop(0, points, solve, 0)

    for piece in range(early, held):
        for cut in range(cuts):
            send, keep = first_of(piece, held + (piece - early) * cuts + cut, cut=cut)
            keep()
            send_over(send)
            send_within(send)

    for read in reads[5:]:
        read.wait()
    span = total * SUBLANES
    column = lax.broadcasted_iota(jnp.int32, (SUBLANES, span), 1)
    lane_slot = lax.rem(column, SUBLANES)
    lane_point = lax.div(column, SUBLANES)
    same = lane_slot == lax.broadcasted_iota(jnp.int32, (SUBLANES, span), 0)

    def place(index, carried):
        return jnp.where(lane_point == index, energy_ref[index], carried)

    column_energy = lax.fori_loop(0, total, place, jnp.zeros((SUBLANES, span), jnp.float32))

    def build(index, carried):
        spacing = energy_ref[index] - column_energy
        row = lorentz(spacing - PHONON) + lorentz(spacing + PHONON)
        row = jnp.where(same, row, 0.0)
        row = row * (MIX_RATE / jnp.sum(row, axis=1, keepdims=True))
        wide[pl.ds(pl.multiple_of(index * SUBLANES, SUBLANES), SUBLANES), :] = row
        return carried

    lax.fori_loop(0, total, build, 0)
    weights = []
    for step in range(moments):
        weight = jnp.float32(0.0)
        for transfer in range(strength_ref.shape[0]):
            weight = weight + jnp.where(offset_ref[transfer] == step, strength_ref[transfer], 0.0)
        weights.append(weight)

    wide_parts = left_parts(wide[...])
    arrivals = [(piece, None) for piece in range(early)] + [
        (piece, cut) for piece in range(early, held) for cut in range(cuts)
    ]

    def settle(landed, semaphore):
        pltpu.make_async_copy(landed, landed, recv_first.at[semaphore]).wait()

    for piece, cut in arrivals:
        if cut is None:
            chosen = slice(None)
            settle(gathered.at[:, piece], piece)
        else:
            chosen = slice(cut * width, (cut + 1) * width)
            if cut == 0:
                settle(gathered.at[:, piece, pl.ds(0, ranks)], piece)
            settle(
                gathered.at[:, piece, pl.ds(0, total - ranks), :, chosen],
                held + (piece - early) * cuts + cut,
            )
        for moment in range(moments):
            scattered = weights[0] * gathered[moment, piece, :, :, chosen]
            for step in range(1, moments):
                source = (moment - step) % moments
                scattered = scattered + weights[step] * gathered[source, piece, :, :, chosen]
            columns = scattered.shape[-1]
            result = multiply(wide_parts, right_parts(scattered.reshape(span, columns)))
            mixed_out[moment, piece, :, :, chosen] = result.reshape(total, SUBLANES, columns)

        def give_back(other, piece=piece, chosen=chosen):
            rank = other // moments
            pltpu.make_async_remote_copy(
                src_ref=mixed_out.at[lax.rem(other, moments), piece, pl.ds(rank * points, points), :, chosen],
                dst_ref=out_ref.at[:, tile_of(me, piece), :, chosen],
                send_sem=send_second,
                recv_sem=recv_second,
                device_id=place_of(other),
                device_id_type=MESH_ID,
            ).start()

        send_over(give_back)
        send_within(give_back)
        pltpu.make_async_copy(
            mixed_out.at[my_moment, piece, pl.ds(my_rank * points, points), :, chosen],
            out_ref.at[:, tile_of(me, piece), :, chosen],
            recv_second,
        ).start()

    pltpu.make_async_copy(out_ref, out_ref, recv_second).wait()
    sent = green.at[:, pl.ds(0, (devices - 1) * held)]
    pltpu.make_async_copy(sent, sent, send_first).wait()
    pltpu.make_async_copy(sent, sent, send_second).wait()


def fused_body(sigma_in, hamiltonian, coupling, energies, counts, strengths, offsets):
    points, order = sigma_in.shape[0], sigma_in.shape[3]
    ranks = lax.axis_size("energy")
    moments = lax.axis_size("mom")
    tiles = 2 * order // SUBLANES
    held = tiles // (ranks * moments)
    total = ranks * points
    span = total * SUBLANES
    cuts = 2 if order % 256 == 0 else 1
    hbm = pl.BlockSpec(memory_space=pltpu.HBM)
    operands = (energies, counts, strengths, offsets, sigma_in[:, 0], hamiltonian[0], coupling[0])
    sigma_new, sigma_held = pl.pallas_call(
        functools.partial(kernel, ranks, moments, points, order, held),
        out_shape=[
            jax.ShapeDtypeStruct((points, tiles, SUBLANES, order), jnp.float32),
            jax.ShapeDtypeStruct((points, 2, order, order), jnp.float32),
        ],
        in_specs=[hbm] * 7,
        out_specs=[pl.BlockSpec(memory_space=pltpu.VMEM)] * 2,
        scratch_shapes=[
            pltpu.VMEM((points, tiles, SUBLANES, order), jnp.float32),
            pltpu.VMEM((moments, held, total, SUBLANES, order), jnp.float32),
            pltpu.VMEM((moments, held, total, SUBLANES, order), jnp.float32),
            pltpu.VMEM((span, span), jnp.float32),
            pltpu.VMEM((2, order, order), jnp.bfloat16),
            pltpu.VMEM((2, order, order), jnp.bfloat16),
            pltpu.VMEM((2, order, order), jnp.float32),
            pltpu.VMEM((order, order), jnp.float32),
            pltpu.SMEM(energies.shape, jnp.float32),
            pltpu.SMEM(counts.shape, jnp.int32),
            pltpu.SMEM(strengths.shape, jnp.float32),
            pltpu.SMEM(offsets.shape, jnp.int32),
            pltpu.SemaphoreType.REGULAR,
            pltpu.SemaphoreType.DMA((points, 2)),
            pltpu.SemaphoreType.DMA((7,)),
            pltpu.SemaphoreType.DMA,
            pltpu.SemaphoreType.DMA((held + held // 2 * cuts,)),
            pltpu.SemaphoreType.DMA,
            pltpu.SemaphoreType.DMA,
        ],
        compiler_params=pltpu.CompilerParams(
            collective_id=0, has_side_effects=True, vmem_limit_bytes=32 * 1024 * 1024
        ),
        name="green_and_scatter",
    )(*[pltpu.with_memory_space_constraint(value, pltpu.HBM) for value in operands])
    result = (1.0 - MIX_RATE) * sigma_held.reshape(sigma_in.shape) + sigma_new.reshape(sigma_in.shape)
    return result


def body(sigma_in, hamiltonian, coupling, energies, counts, strengths, offsets):
    devices = lax.axis_size("energy") * lax.axis_size("mom")
    tiles = 2 * sigma_in.shape[3] // SUBLANES
    fits = tiles % (2 * devices) == 0 and lax.axis_size("energy") % 8 == 0 and sigma_in.shape[0] > 1
    chosen = fused_body if fits else plain_body
    return chosen(sigma_in, hamiltonian, coupling, energies, counts, strengths, offsets)


def solution(mesh):
    placed = (
        P("energy", "mom", None, None, None),
        P("mom", None, None, None),
        P("mom", None, None),
        P(),
        P(),
        P(),
        P(),
    )
    return jax.shard_map(
        body,
        mesh=mesh,
        in_specs=placed,
        out_specs=P("energy", "mom", None, None, None),
        check_vma=False,
    )
```

```python
import functools

import jax
import jax.numpy as jnp
from jax import lax
from jax.experimental import pallas as pl
from jax.experimental.pallas import tpu as pltpu
from jax.sharding import PartitionSpec as P

PRECISE = lax.Precision.HIGHEST
MIX_RATE = 0.6
PHONON = 0.1
BROADENING = 0.02


def shifted(value, axis, steps):
    count = lax.axis_size(axis)
    pairs = [(source, (source + steps) % count) for source in range(count)]
    return lax.ppermute(value, axis, pairs)


def product(left_side, right_side):
    return jnp.dot(left_side, right_side, precision=PRECISE, preferred_element_type=jnp.float32)


def invert(matrix, energy, sweeps):
    identity = jnp.eye(matrix.shape[0], dtype=jnp.float32)

    def keep_going(carried):
        return carried[0] < sweeps

    def sweep(carried):
        estimate = carried[1]
        return (carried[0] + 1, 2.0 * estimate - product(estimate, product(matrix, estimate)))

    return lax.while_loop(keep_going, sweep, (jnp.int32(0), identity / energy))[1]


def solve_point(ham_block, coupling_block, sigma_pair, energy, sweeps):
    identity = jnp.eye(ham_block.shape[1], dtype=jnp.float32)
    left_matrix = energy * identity - ham_block[0] - sigma_pair[0]
    left_inverse = invert(left_matrix, energy, sweeps)
    inverse_coupled = product(left_inverse, coupling_block)
    coupled_inverse = product(coupling_block.T, left_inverse)
    right_matrix = (
        energy * identity
        - ham_block[1]
        - sigma_pair[1]
        - product(coupling_block.T, inverse_coupled)
    )
    right_green = invert(right_matrix, energy, sweeps)
    left_green = left_inverse + product(product(inverse_coupled, right_green), coupled_inverse)
    return jnp.stack([left_green, right_green])


def lorentz(offset):
    scaled = offset / BROADENING
    return 1.0 / (1.0 + scaled * scaled)


def build_kernel(row_energy, column_energy):
    spacing = row_energy[:, None] - column_energy[None, :]
    kernel = lorentz(spacing - PHONON) + lorentz(spacing + PHONON)
    return kernel / jnp.sum(kernel, axis=1, keepdims=True)


def plain_body(sigma_in, hamiltonian, coupling, energies, counts, strengths, offsets):
    points = sigma_in.shape[0]
    order = sigma_in.shape[3]
    ranks = lax.axis_size("energy")
    moments = lax.axis_size("mom")
    my_rank = lax.axis_index("energy")
    own_energy = lax.dynamic_slice_in_dim(energies, my_rank * points, points)
    own_count = lax.dynamic_slice_in_dim(counts, my_rank * points, points)
    blocks = sigma_in[:, 0]

    def solve_held(held_point):
        return solve_point(hamiltonian[0], coupling[0], held_point[0], held_point[1], held_point[2])

    green_blocks = lax.map(solve_held, (blocks, own_energy, own_count))
    shift_index = jnp.arange(moments, dtype=jnp.int32)
    weights = jnp.sum(
        strengths[:, None] * (offsets[:, None] == shift_index[None, :]).astype(jnp.float32), axis=0
    )
    kernel = build_kernel(energies, energies)
    piece_width = 2 * order * order // ranks
    spread = green_blocks.reshape(points, ranks, moments, piece_width // moments)
    column = lax.all_to_all(spread, "energy", split_axis=1, concat_axis=0, tiled=True)[:, 0]
    rows_all = column.shape[0]
    flat_column = column.reshape(rows_all, -1)
    mixed_sum = weights[0] * flat_column
    for offset_step in range(1, moments):
        mixed_sum = mixed_sum + weights[offset_step] * shifted(flat_column, "mom", offset_step)
    sigma_part = product(kernel, mixed_sum).reshape(column.shape)
    result = lax.all_to_all(sigma_part[:, None], "energy", split_axis=0, concat_axis=1, tiled=True)
    sigma_new = result.reshape(sigma_in.shape)
    return (1.0 - MIX_RATE) * sigma_in + MIX_RATE * sigma_new


SUBLANES = 8
MESH_ID = pl.DeviceIdType.MESH


def split(value):
    high = value.astype(jnp.bfloat16)
    return high, (value - high.astype(jnp.float32)).astype(jnp.bfloat16)


left_parts = right_parts = split


def multiply(left_side, right_side):
    (high, low), (near, far) = left_side, right_side
    rows = high.shape[0] // 2
    both = [
        jnp.dot(jnp.concatenate([high[n * rows:(n + 1) * rows], low[n * rows:(n + 1) * rows]], axis=0), near, preferred_element_type=jnp.float32)
        for n in range(2)
    ]
    last = [jnp.dot(high[n * rows:(n + 1) * rows], far, preferred_element_type=jnp.float32) for n in range(2)]
    return jnp.concatenate([b[:rows] + b[rows:] + l for b, l in zip(both, last)], axis=0)


def series(ratio, energy, count, identity):
    square = multiply(left_parts(ratio), right_parts(ratio))
    total = identity + ratio
    right = right_parts(square)
    fourth = multiply(left_parts(square), right)
    short = total + multiply(left_parts(total), right)
    right = right_parts(fourth)
    eighth = multiply(left_parts(fourth), right)
    total = short + multiply(left_parts(short), right)
    total = total + multiply(left_parts(total), right_parts(eighth))
    return jnp.where(count > 2, total, short) * (1.0 / energy)


def powers(ratio, count, identity, prepare):
    square = multiply(left_parts(ratio), right_parts(ratio))
    prepare()
    total = identity + ratio
    right = right_parts(square)
    fourth = multiply(left_parts(square), right)
    short = total + multiply(left_parts(total), right)
    fourth = jnp.where(count > 2, fourth, 0.0)
    right = right_parts(fourth)
    eighth = multiply(left_parts(fourth), right)
    total = short + multiply(left_parts(short), right)
    return total, eighth


def kernel(
    ranks, moments, points, order, held,
    energy_hbm, count_hbm, strength_hbm, offset_hbm, sigma_hbm, ham_hbm, coupling_hbm,
    out_ref, sigma_ref,
    green, gathered, mixed_out, wide, across, across_t,
    ham_ref, coupling_ref, energy_ref, count_ref, strength_ref, offset_ref,
    ready, read_sigma, read_other, send_first, recv_first, send_second, recv_second,
):
    devices = ranks * moments
    side = devices // 2
    group = side // 2
    total = ranks * points
    early = held // 2
    cuts = 2 if order % 256 == 0 else 1
    width = order // cuts
    my_rank = lax.axis_index("energy")
    my_moment = lax.axis_index("mom")
    me = my_rank * moments + my_moment
    my_side = me // side
    spot = lax.rem(me, side)
    near_side = my_side * side
    far_side = (1 - my_side) * side

    def place_of(other):
        return {"energy": other // moments, "mom": lax.rem(other, moments)}

    sources = [
        (coupling_hbm, coupling_ref), (ham_hbm.at[0], ham_ref.at[0]), (ham_hbm.at[1], ham_ref.at[1]),
        (energy_hbm, energy_ref), (count_hbm, count_ref), (strength_hbm, strength_ref), (offset_hbm, offset_ref),
    ]
    reads = [pltpu.make_async_copy(a, b, read_other.at[n]) for n, (a, b) in enumerate(sources)]

    def sigma_read(point, slab):
        return pltpu.make_async_copy(
            sigma_hbm.at[point, slab], sigma_ref.at[point, slab], read_sigma.at[point, slab]
        )

    for read in [reads[1], sigma_read(0, 0), reads[3], reads[4]]:
        read.start()
    barrier = pltpu.get_barrier_semaphore()

    quarter = ranks // 4
    blocks = quarter // 2
    my_block = lax.rem(lax.div(my_rank, 2), blocks)
    my_core = lax.rem(my_rank, 2)

    def send_over(send):
        def over(index, carried):
            turn = lax.div(index, group)
            layer = turn * my_side + (1 - turn) * (1 - my_side)
            step = group - 1 - lax.rem(index, group)
            block = lax.rem(my_block + lax.div(step, 2 * moments), blocks)
            moment = lax.rem(my_moment + lax.rem(lax.div(step, 2), moments), moments)
            core = lax.rem(my_core + lax.rem(step, 2), 2)
            rank = (1 - my_side) * (ranks // 2) + layer * quarter + block * 2 + core
            send(rank * moments + moment)
            return carried

        lax.fori_loop(0, side, over, 0)

    def greet(other):
        pl.semaphore_signal(barrier, inc=1, device_id=place_of(other), device_id_type=MESH_ID)

    send_over(greet)
    for read in [reads[0], reads[2], sigma_read(0, 1)]:
        read.start()

    row_index = lax.broadcasted_iota(jnp.int32, (order, order), 0)
    identity = (row_index == lax.broadcasted_iota(jnp.int32, (order, order), 1)).astype(jnp.float32)

    def tile_of(other, piece):
        return (held - 1 - piece) * devices + other

    def send_within(send):
        def within(index, carried):
            send(near_side + lax.rem(spot + index, side))
            return carried

        lax.fori_loop(1, side, within, 0)

    def first_of(piece, semaphore, point=None, cut=None):
        if cut is None:
            landing = gathered.at[my_moment, piece, my_rank * points + point]
            source_of = lambda other: green.at[point, tile_of(other, piece)]
        else:
            later, chosen = pl.ds(1, points - 1), pl.ds(cut * width, width)
            landing = gathered.at[my_moment, piece, pl.ds(my_rank * points + 1, points - 1), :, chosen]
            source_of = lambda other: green.at[later, tile_of(other, piece), :, chosen]

        def send(other):
            pltpu.make_async_remote_copy(
                src_ref=source_of(other), dst_ref=landing,
                send_sem=send_first, recv_sem=recv_first.at[semaphore],
                device_id=place_of(other), device_id_type=MESH_ID,
            ).start()

        def keep():
            pltpu.make_async_copy(source_of(me), landing, recv_first.at[semaphore]).start()

        return send, keep

    for read in [reads[3], reads[4], reads[1], sigma_read(0, 0)]:
        read.wait()
    tiles = order // SUBLANES

    def solve(point, first):
        if not first:
            sigma_read(point, 0).wait()
            sigma_read(point, 1).wait()
        energy = energy_ref[my_rank * points + point]
        count = count_ref[my_rank * points + point]
        ratio = (ham_ref[0] + sigma_ref[point, 0]) * (1.0 / energy)

        def prepare():
            if first:
                reads[0].wait()
                across[0], across[1] = split(coupling_ref[...])
                across_t[0], across_t[1] = split(coupling_ref[...].T)

        total, last = powers(ratio, count, identity, prepare)
        spread = coupling_ref[...] + multiply(left_parts(last), (across[0], across[1]))
        back = multiply((across_t[0], across_t[1]), right_parts(total))

        fold = multiply(left_parts(back), right_parts(spread)) * (1.0 / energy)
        if first:
            reads[2].wait()
            sigma_read(0, 1).wait()
        ratio = (ham_ref[1] + sigma_ref[point, 1] + fold) * (1.0 / energy)
        right_green = series(ratio, energy, count, identity)
        green[point, tiles:] = right_green.reshape(tiles, SUBLANES, order)

        if first:
            pl.semaphore_wait(barrier, side)
            mirror = lax.rem(me + side, devices)
            pl.semaphore_signal(ready, inc=1, device_id=place_of(mirror), device_id_type=MESH_ID)

        for piece in range(early):
            send_over(first_of(piece, piece, point=point)[0])
        if first:
            for read in reads[5:]:
                read.start()

            def read_point(point, carried):
                sigma_read(point, 0).start()
                sigma_read(point, 1).start()
                return carried

            lax.fori_loop(1, points, read_point, 0)
        else:

            @pl.when(point == 1)
            def _():
                pl.semaphore_wait(ready, 1)
                for piece in range(held):
                    send, keep = first_of(piece, piece, point=0)
                    keep()
                    send_within(send)

        right = right_parts(last)
        left_inverse = (total + multiply(left_parts(total), right)) * (1.0 / energy)
        back = (back + multiply(left_parts(back), right)) * (1.0 / energy)
        coupled = multiply(left_parts(total), right_parts(spread)) * (1.0 / energy)
        inner = multiply(left_parts(coupled), right_parts(right_green))
        left_green = left_inverse + multiply(left_parts(inner), right_parts(back))
        green[point, :tiles] = left_green.reshape(tiles, SUBLANES, order)

        if first:
            for piece in range(early, held):
                send_over(first_of(piece, piece, point=0)[0])
        else:
            for piece in range(early):
                send, keep = first_of(piece, piece, point=point)
                keep()
                send_within(send)

    def solve_later(point, carried):
        solve(point, False)
        return carried

    solve(0, True)
    lax.fori_loop(1, points, solve_later, 0)

    for piece in range(early, held):
        for cut in range(cuts):
            send, keep = first_of(piece, held + (piece - early) * cuts + cut, cut=cut)
            keep()
            send_over(send)
            send_within(send)

    for read in reads[5:]:
        read.wait()
    span = total * SUBLANES
    column = lax.broadcasted_iota(jnp.int32, (SUBLANES, span), 1)
    lane_slot = lax.rem(column, SUBLANES)
    lane_point = lax.div(column, SUBLANES)
    same = lane_slot == lax.broadcasted_iota(jnp.int32, (SUBLANES, span), 0)

    def place(index, carried):
        return jnp.where(lane_point == index, energy_ref[index], carried)

    column_energy = lax.fori_loop(0, total, place, jnp.zeros((SUBLANES, span), jnp.float32))

    def build(index, carried):
        spacing = energy_ref[index] - column_energy
        row = lorentz(spacing - PHONON) + lorentz(spacing + PHONON)
        row = jnp.where(same, row, 0.0)
        row = row * (MIX_RATE / jnp.sum(row, axis=1, keepdims=True))
        wide[pl.ds(pl.multiple_of(index * SUBLANES, SUBLANES), SUBLANES), :] = row
        return carried

    lax.fori_loop(0, total, build, 0)
    weights = []
    for step in range(moments):
        weight = jnp.float32(0.0)
        for transfer in range(strength_ref.shape[0]):
            weight = weight + jnp.where(offset_ref[transfer] == step, strength_ref[transfer], 0.0)
        weights.append(weight)

    wide_parts = left_parts(wide[...])
    arrivals = [(piece, None) for piece in range(early)] + [
        (piece, cut) for piece in range(early, held) for cut in range(cuts)
    ]

    def settle(landed, semaphore):
        pltpu.make_async_copy(landed, landed, recv_first.at[semaphore]).wait()

    for piece, cut in arrivals:
        if cut is None:
            chosen = slice(None)
            settle(gathered.at[:, piece], piece)
        else:
            chosen = slice(cut * width, (cut + 1) * width)
            if cut == 0:
                settle(gathered.at[:, piece, pl.ds(0, ranks)], piece)
            settle(
                gathered.at[:, piece, pl.ds(0, total - ranks), :, chosen],
                held + (piece - early) * cuts + cut,
            )
        for moment in range(moments):
            scattered = weights[0] * gathered[moment, piece, :, :, chosen]
            for step in range(1, moments):
                source = (moment - step) % moments
                scattered = scattered + weights[step] * gathered[source, piece, :, :, chosen]
            columns = scattered.shape[-1]
            result = multiply(wide_parts, right_parts(scattered.reshape(span, columns)))
            mixed_out[moment, piece, :, :, chosen] = result.reshape(total, SUBLANES, columns)

        def give_back(other, piece=piece, chosen=chosen):
            rank = other // moments
            pltpu.make_async_remote_copy(
                src_ref=mixed_out.at[lax.rem(other, moments), piece, pl.ds(rank * points, points), :, chosen],
                dst_ref=out_ref.at[:, tile_of(me, piece), :, chosen],
                send_sem=send_second,
                recv_sem=recv_second,
                device_id=place_of(other),
                device_id_type=MESH_ID,
            ).start()

        send_over(give_back)
        send_within(give_back)
        pltpu.make_async_copy(
            mixed_out.at[my_moment, piece, pl.ds(my_rank * points, points), :, chosen],
            out_ref.at[:, tile_of(me, piece), :, chosen],
            recv_second,
        ).start()

    pltpu.make_async_copy(out_ref, out_ref, recv_second).wait()
    sent = green.at[:, pl.ds(0, (devices - 1) * held)]
    pltpu.make_async_copy(sent, sent, send_first).wait()
    pltpu.make_async_copy(sent, sent, send_second).wait()


def finish(parts, sigma_ref, new_ref, out_hbm, mixed, done):
    rows = sigma_ref.shape[0] // parts
    copies = []
    for part in range(parts):
        chosen = pl.ds(part * rows, rows)
        mixed[chosen] = (1.0 - MIX_RATE) * sigma_ref[chosen] + new_ref[chosen]
        copy = pltpu.make_async_copy(mixed.at[chosen], out_hbm.at[chosen], done.at[part])
        copy.start()
        copies.append(copy)
    for copy in copies:
        copy.wait()


def fused_body(sigma_in, hamiltonian, coupling, energies, counts, strengths, offsets):
    points, order = sigma_in.shape[0], sigma_in.shape[3]
    ranks = lax.axis_size("energy")
    moments = lax.axis_size("mom")
    tiles = 2 * order // SUBLANES
    held = tiles // (ranks * moments)
    total = ranks * points
    span = total * SUBLANES
    cuts = 2 if order % 256 == 0 else 1
    hbm = pl.BlockSpec(memory_space=pltpu.HBM)
    operands = (energies, counts, strengths, offsets, sigma_in[:, 0], hamiltonian[0], coupling[0])
    sigma_new, sigma_held = pl.pallas_call(
        functools.partial(kernel, ranks, moments, points, order, held),
        out_shape=[
            jax.ShapeDtypeStruct((points, tiles, SUBLANES, order), jnp.float32),
            jax.ShapeDtypeStruct((points, 2, order, order), jnp.float32),
        ],
        in_specs=[hbm] * 7,
        out_specs=[pl.BlockSpec(memory_space=pltpu.VMEM)] * 2,
        scratch_shapes=[
            pltpu.VMEM((points, tiles, SUBLANES, order), jnp.float32),
            pltpu.VMEM((moments, held, total, SUBLANES, order), jnp.float32),
            pltpu.VMEM((moments, held, total, SUBLANES, order), jnp.float32),
            pltpu.VMEM((span, span), jnp.float32),
            pltpu.VMEM((2, order, order), jnp.bfloat16),
            pltpu.VMEM((2, order, order), jnp.bfloat16),
            pltpu.VMEM((2, order, order), jnp.float32),
            pltpu.VMEM((order, order), jnp.float32),
            pltpu.SMEM(energies.shape, jnp.float32),
            pltpu.SMEM(counts.shape, jnp.int32),
            pltpu.SMEM(strengths.shape, jnp.float32),
            pltpu.SMEM(offsets.shape, jnp.int32),
            pltpu.SemaphoreType.REGULAR,
            pltpu.SemaphoreType.DMA((points, 2)),
            pltpu.SemaphoreType.DMA((7,)),
            pltpu.SemaphoreType.DMA,
            pltpu.SemaphoreType.DMA((held + held // 2 * cuts,)),
            pltpu.SemaphoreType.DMA,
            pltpu.SemaphoreType.DMA,
        ],
        compiler_params=pltpu.CompilerParams(
            collective_id=0, has_side_effects=True, vmem_limit_bytes=32 * 1024 * 1024
        ),
        name="green_and_scatter",
    )(*[pltpu.with_memory_space_constraint(value, pltpu.HBM) for value in operands])
    cells = (points * tiles, SUBLANES, order)
    vmem = pl.BlockSpec(memory_space=pltpu.VMEM)
    parts = 4
    result = pl.pallas_call(
        functools.partial(finish, parts),
        out_shape=jax.ShapeDtypeStruct(cells, jnp.float32),
        in_specs=[vmem] * 2,
        out_specs=pl.BlockSpec(memory_space=pltpu.HBM),
        scratch_shapes=[pltpu.VMEM(cells, jnp.float32), pltpu.SemaphoreType.DMA((parts,))],
        compiler_params=pltpu.CompilerParams(vmem_limit_bytes=8 * 1024 * 1024),
        name="mix",
    )(sigma_held.reshape(cells), sigma_new.reshape(cells))
    return result.reshape(sigma_in.shape)


def body(sigma_in, hamiltonian, coupling, energies, counts, strengths, offsets):
    devices = lax.axis_size("energy") * lax.axis_size("mom")
    tiles = 2 * sigma_in.shape[3] // SUBLANES
    fits = tiles % (2 * devices) == 0 and lax.axis_size("energy") % 8 == 0 and sigma_in.shape[0] > 1
    chosen = fused_body if fits else plain_body
    return chosen(sigma_in, hamiltonian, coupling, energies, counts, strengths, offsets)


def solution(mesh):
    placed = (
        P("energy", "mom", None, None, None),
        P("mom", None, None, None),
        P("mom", None, None),
        P(),
        P(),
        P(),
        P(),
    )
    return jax.shard_map(
        body,
        mesh=mesh,
        in_specs=placed,
        out_specs=P("energy", "mom", None, None, None),
        check_vma=False,
    )
```

```python
import functools

import jax
import jax.numpy as jnp
from jax import lax
from jax.experimental import pallas as pl
from jax.experimental.pallas import tpu as pltpu
from jax.sharding import PartitionSpec as P

PRECISE = lax.Precision.HIGHEST
MIX_RATE = 0.6
PHONON = 0.1
BROADENING = 0.02


def shifted(value, axis, steps):
    count = lax.axis_size(axis)
    pairs = [(source, (source + steps) % count) for source in range(count)]
    return lax.ppermute(value, axis, pairs)


def product(left_side, right_side):
    return jnp.dot(left_side, right_side, precision=PRECISE, preferred_element_type=jnp.float32)


def invert(matrix, energy, sweeps):
    identity = jnp.eye(matrix.shape[0], dtype=jnp.float32)

    def keep_going(carried):
        return carried[0] < sweeps

    def sweep(carried):
        estimate = carried[1]
        return (carried[0] + 1, 2.0 * estimate - product(estimate, product(matrix, estimate)))

    return lax.while_loop(keep_going, sweep, (jnp.int32(0), identity / energy))[1]


def solve_point(ham_block, coupling_block, sigma_pair, energy, sweeps):
    identity = jnp.eye(ham_block.shape[1], dtype=jnp.float32)
    left_matrix = energy * identity - ham_block[0] - sigma_pair[0]
    left_inverse = invert(left_matrix, energy, sweeps)
    inverse_coupled = product(left_inverse, coupling_block)
    coupled_inverse = product(coupling_block.T, left_inverse)
    right_matrix = (
        energy * identity
        - ham_block[1]
        - sigma_pair[1]
        - product(coupling_block.T, inverse_coupled)
    )
    right_green = invert(right_matrix, energy, sweeps)
    left_green = left_inverse + product(product(inverse_coupled, right_green), coupled_inverse)
    return jnp.stack([left_green, right_green])


def lorentz(offset):
    scaled = offset / BROADENING
    return 1.0 / (1.0 + scaled * scaled)


def build_kernel(row_energy, column_energy):
    spacing = row_energy[:, None] - column_energy[None, :]
    kernel = lorentz(spacing - PHONON) + lorentz(spacing + PHONON)
    return kernel / jnp.sum(kernel, axis=1, keepdims=True)


def plain_body(sigma_in, hamiltonian, coupling, energies, counts, strengths, offsets):
    points = sigma_in.shape[0]
    order = sigma_in.shape[3]
    ranks = lax.axis_size("energy")
    moments = lax.axis_size("mom")
    my_rank = lax.axis_index("energy")
    own_energy = lax.dynamic_slice_in_dim(energies, my_rank * points, points)
    own_count = lax.dynamic_slice_in_dim(counts, my_rank * points, points)
    blocks = sigma_in[:, 0]

    def solve_held(held_point):
        return solve_point(hamiltonian[0], coupling[0], held_point[0], held_point[1], held_point[2])

    green_blocks = lax.map(solve_held, (blocks, own_energy, own_count))
    shift_index = jnp.arange(moments, dtype=jnp.int32)
    weights = jnp.sum(
        strengths[:, None] * (offsets[:, None] == shift_index[None, :]).astype(jnp.float32), axis=0
    )
    kernel = build_kernel(energies, energies)
    piece_width = 2 * order * order // ranks
    spread = green_blocks.reshape(points, ranks, moments, piece_width // moments)
    column = lax.all_to_all(spread, "energy", split_axis=1, concat_axis=0, tiled=True)[:, 0]
    rows_all = column.shape[0]
    flat_column = column.reshape(rows_all, -1)
    mixed_sum = weights[0] * flat_column
    for offset_step in range(1, moments):
        mixed_sum = mixed_sum + weights[offset_step] * shifted(flat_column, "mom", offset_step)
    sigma_part = product(kernel, mixed_sum).reshape(column.shape)
    result = lax.all_to_all(sigma_part[:, None], "energy", split_axis=0, concat_axis=1, tiled=True)
    sigma_new = result.reshape(sigma_in.shape)
    return (1.0 - MIX_RATE) * sigma_in + MIX_RATE * sigma_new


SUBLANES = 8
MESH_ID = pl.DeviceIdType.MESH


def split(value):
    high = value.astype(jnp.bfloat16)
    return high, (value - high.astype(jnp.float32)).astype(jnp.bfloat16)


left_parts = right_parts = split


def multiply(left_side, right_side):
    (high, low), (near, far) = left_side, right_side
    rows = high.shape[0] // 2
    both = [
        jnp.dot(jnp.concatenate([low[n * rows:(n + 1) * rows], high[n * rows:(n + 1) * rows]], axis=0), near, preferred_element_type=jnp.float32)
        for n in range(2)
    ]
    last = [jnp.dot(high[n * rows:(n + 1) * rows], far, preferred_element_type=jnp.float32) for n in range(2)]
    return jnp.concatenate([b[:rows] + l + b[rows:] for b, l in zip(both, last)], axis=0)


def series(ratio, energy, count, identity):
    square = multiply(left_parts(ratio), right_parts(ratio))
    total = identity + ratio
    right = right_parts(square)
    fourth = multiply(left_parts(square), right)
    short = total + multiply(left_parts(total), right)
    right = right_parts(fourth)
    eighth = multiply(left_parts(fourth), right)
    total = short + multiply(left_parts(short), right)
    total = total + multiply(left_parts(total), right_parts(eighth))
    return jnp.where(count > 2, total, short) * (1.0 / energy)


def powers(ratio, count, identity, prepare):
    square = multiply(left_parts(ratio), right_parts(ratio))
    prepare()
    total = identity + ratio
    right = right_parts(square)
    fourth = multiply(left_parts(square), right)
    short = total + multiply(left_parts(total), right)
    fourth = jnp.where(count > 2, fourth, 0.0)
    right = right_parts(fourth)
    eighth = multiply(left_parts(fourth), right)
    total = short + multiply(left_parts(short), right)
    return total, eighth


def kernel(
    ranks, moments, points, order, held,
    energy_hbm, count_hbm, strength_hbm, offset_hbm, sigma_hbm, ham_hbm, coupling_hbm,
    out_ref, sigma_ref,
    green, gathered, mixed_out, wide, across, across_t,
    ham_ref, coupling_ref, energy_ref, count_ref, strength_ref, offset_ref,
    ready, read_sigma, read_other, send_first, recv_first, send_second, recv_second,
):
    devices = ranks * moments
    side = devices // 2
    group = side // 2
    total = ranks * points
    early = held // 2
    cuts = 2 if order % 256 == 0 else 1
    width = order // cuts
    my_rank = lax.axis_index("energy")
    my_moment = lax.axis_index("mom")
    me = my_rank * moments + my_moment
    my_side = me // side
    spot = lax.rem(me, side)
    near_side = my_side * side
    far_side = (1 - my_side) * side

    def place_of(other):
        return {"energy": other // moments, "mom": lax.rem(other, moments)}

    sources = [
        (coupling_hbm, coupling_ref), (ham_hbm.at[0], ham_ref.at[0]), (ham_hbm.at[1], ham_ref.at[1]),
        (energy_hbm, energy_ref), (count_hbm, count_ref), (strength_hbm, strength_ref), (offset_hbm, offset_ref),
    ]
    reads = [pltpu.make_async_copy(a, b, read_other.at[n]) for n, (a, b) in enumerate(sources)]

    def sigma_read(point, slab):
        return pltpu.make_async_copy(
            sigma_hbm.at[point, slab], sigma_ref.at[point, slab], read_sigma.at[point, slab]
        )

    for read in [reads[1], sigma_read(0, 0), reads[3], reads[4]]:
        read.start()
    barrier = pltpu.get_barrier_semaphore()

    quarter = ranks // 4
    blocks = quarter // 2
    my_block = lax.rem(lax.div(my_rank, 2), blocks)
    my_core = lax.rem(my_rank, 2)

    def send_over(send, begin=0, end=side):
        def over(index, carried):
            turn = lax.div(index, group)
            layer = turn * my_side + (1 - turn) * (1 - my_side)
            step = group - 1 - lax.rem(index, group)
            block = lax.rem(my_block + lax.div(step, 2 * moments), blocks)
            moment = lax.rem(my_moment + lax.rem(lax.div(step, 2), moments), moments)
            core = lax.rem(my_core + lax.rem(step, 2), 2)
            rank = (1 - my_side) * (ranks // 2) + layer * quarter + block * 2 + core
            send(rank * moments + moment)
            return carried

        lax.fori_loop(begin, end, over, 0)

    def greet(other):
        pl.semaphore_signal(barrier, inc=1, device_id=place_of(other), device_id_type=MESH_ID)

    send_over(greet)
    for read in [reads[0], reads[2], sigma_read(0, 1)]:
        read.start()

    row_index = lax.broadcasted_iota(jnp.int32, (order, order), 0)
    identity = (row_index == lax.broadcasted_iota(jnp.int32, (order, order), 1)).astype(jnp.float32)

    def tile_of(other, piece):
        return (held - 1 - piece) * devices + other

    def send_within(send):
        def within(index, carried):
            send(near_side + lax.rem(spot + index, side))
            return carried

        lax.fori_loop(1, side, within, 0)

    def first_of(piece, semaphore, point=None, cut=None):
        if cut is None:
            landing = gathered.at[my_moment, piece, my_rank * points + point]
            source_of = lambda other: green.at[point, tile_of(other, piece)]
        else:
            later, chosen = pl.ds(1, points - 1), pl.ds(cut * width, width)
            landing = gathered.at[my_moment, piece, pl.ds(my_rank * points + 1, points - 1), :, chosen]
            source_of = lambda other: green.at[later, tile_of(other, piece), :, chosen]

        def send(other):
            pltpu.make_async_remote_copy(
                src_ref=source_of(other), dst_ref=landing,
                send_sem=send_first, recv_sem=recv_first.at[semaphore],
                device_id=place_of(other), device_id_type=MESH_ID,
            ).start()

        def keep():
            pltpu.make_async_copy(source_of(me), landing, recv_first.at[semaphore]).start()

        return send, keep

    for read in [reads[3], reads[4], reads[1], sigma_read(0, 0)]:
        read.wait()
    tiles = order // SUBLANES

    def solve(point, first):
        if not first:
            sigma_read(point, 0).wait()
            sigma_read(point, 1).wait()
        energy = energy_ref[my_rank * points + point]
        count = count_ref[my_rank * points + point]
        ratio = (ham_ref[0] + sigma_ref[point, 0]) * (1.0 / energy)

        def prepare():
            if first:
                reads[0].wait()
                across[0], across[1] = split(coupling_ref[...])
                across_t[0], across_t[1] = split(coupling_ref[...].T)

        total, last = powers(ratio, count, identity, prepare)
        spread = coupling_ref[...] + multiply(left_parts(last), (across[0], across[1]))
        back = multiply((across_t[0], across_t[1]), right_parts(total))

        fold = multiply(left_parts(back), right_parts(spread)) * (1.0 / energy)
        if first:
            reads[2].wait()
            sigma_read(0, 1).wait()
        ratio = (ham_ref[1] + sigma_ref[point, 1] + fold) * (1.0 / energy)
        right_green = series(ratio, energy, count, identity)
        green[point, tiles:] = right_green.reshape(tiles, SUBLANES, order)

        if first:
            pl.semaphore_wait(barrier, side)
            mirror = lax.rem(me + side, devices)
            pl.semaphore_signal(ready, inc=1, device_id=place_of(mirror), device_id_type=MESH_ID)

        for piece in range(early):
            send_over(first_of(piece, piece, point=point)[0])
        if first:
            for read in reads[5:]:
                read.start()

            def read_point(point, carried):
                sigma_read(point, 0).start()
                sigma_read(point, 1).start()
                return carried

            lax.fori_loop(1, points, read_point, 0)
        else:

            @pl.when(point == 1)
            def _():
                pl.semaphore_wait(ready, 1)
                for piece in range(held):
                    send, keep = first_of(piece, piece, point=0)
                    keep()
                    send_within(send)

        right = right_parts(last)
        left_inverse = (total + multiply(left_parts(total), right)) * (1.0 / energy)
        back = (back + multiply(left_parts(back), right)) * (1.0 / energy)
        coupled = multiply(left_parts(total), right_parts(spread)) * (1.0 / energy)
        inner = multiply(left_parts(coupled), right_parts(right_green))
        left_green = left_inverse + multiply(left_parts(inner), right_parts(back))
        green[point, :tiles] = left_green.reshape(tiles, SUBLANES, order)

        if first:
            for piece in range(early, held):
                send_over(first_of(piece, piece, point=0)[0])
        else:
            for piece in range(early):
                send, keep = first_of(piece, piece, point=point)
                keep()
                send_within(send)

    def solve_later(point, carried):
        solve(point, False)
        return carried

    solve(0, True)
    lax.fori_loop(1, points, solve_later, 0)

    for piece in range(early, held):
        for cut in range(cuts):
            send, keep = first_of(piece, held + (piece - early) * cuts + cut, cut=cut)
            keep()
            send_over(send)
            send_within(send)

    for read in reads[5:]:
        read.wait()
    span = total * SUBLANES
    column = lax.broadcasted_iota(jnp.int32, (SUBLANES, span), 1)
    lane_slot = lax.rem(column, SUBLANES)
    lane_point = lax.div(column, SUBLANES)
    same = lane_slot == lax.broadcasted_iota(jnp.int32, (SUBLANES, span), 0)

    def place(index, carried):
        return jnp.where(lane_point == index, energy_ref[index], carried)

    column_energy = lax.fori_loop(0, total, place, jnp.zeros((SUBLANES, span), jnp.float32))

    def build(index, carried):
        spacing = energy_ref[index] - column_energy
        row = lorentz(spacing - PHONON) + lorentz(spacing + PHONON)
        row = jnp.where(same, row, 0.0)
        row = row * (MIX_RATE / jnp.sum(row, axis=1, keepdims=True))
        wide[pl.ds(pl.multiple_of(index * SUBLANES, SUBLANES), SUBLANES), :] = row
        return carried

    lax.fori_loop(0, total, build, 0)
    weights = []
    for step in range(moments):
        weight = jnp.float32(0.0)
        for transfer in range(strength_ref.shape[0]):
            weight = weight + jnp.where(offset_ref[transfer] == step, strength_ref[transfer], 0.0)
        weights.append(weight)

    wide_parts = left_parts(wide[...])
    arrivals = [(piece, None) for piece in range(early)] + [
        (piece, cut) for piece in range(early, held) for cut in range(cuts)
    ]

    waiting = []

    def settle(landed, semaphore):
        pltpu.make_async_copy(landed, landed, recv_first.at[semaphore]).wait()

    for piece, cut in arrivals:
        if cut is None:
            chosen = slice(None)
            settle(gathered.at[:, piece], piece)
        else:
            chosen = slice(cut * width, (cut + 1) * width)
            if cut == 0:
                settle(gathered.at[:, piece, pl.ds(0, ranks)], piece)
            settle(
                gathered.at[:, piece, pl.ds(0, total - ranks), :, chosen],
                held + (piece - early) * cuts + cut,
            )
        for moment in range(moments):
            scattered = weights[0] * gathered[moment, piece, :, :, chosen]
            for step in range(1, moments):
                source = (moment - step) % moments
                scattered = scattered + weights[step] * gathered[source, piece, :, :, chosen]
            columns = scattered.shape[-1]
            result = multiply(wide_parts, right_parts(scattered.reshape(span, columns)))
            mixed_out[moment, piece, :, :, chosen] = result.reshape(total, SUBLANES, columns)

        def give_back(other, piece=piece, chosen=chosen):
            rank = other // moments
            pltpu.make_async_remote_copy(
                src_ref=mixed_out.at[lax.rem(other, moments), piece, pl.ds(rank * points, points), :, chosen],
                dst_ref=out_ref.at[:, tile_of(me, piece), :, chosen],
                send_sem=send_second,
                recv_sem=recv_second,
                device_id=place_of(other),
                device_id_type=MESH_ID,
            ).start()

        held_back = piece == held - 1 and cuts > 1
        if held_back:
            send_over(give_back, 0, group)
        else:
            send_over(give_back)
        send_within(give_back)
        if held_back:
            waiting.append(give_back)
        pltpu.make_async_copy(
            mixed_out.at[my_moment, piece, pl.ds(my_rank * points, points), :, chosen],
            out_ref.at[:, tile_of(me, piece), :, chosen],
            recv_second,
        ).start()

    for give_back in waiting:
        send_over(give_back, group, side)

    pltpu.make_async_copy(out_ref, out_ref, recv_second).wait()
    sent = green.at[:, pl.ds(0, (devices - 1) * held)]
    pltpu.make_async_copy(sent, sent, send_first).wait()
    pltpu.make_async_copy(sent, sent, send_second).wait()


def finish(parts, sigma_ref, new_ref, out_hbm, mixed, done):
    rows = sigma_ref.shape[0] // parts
    copies = []
    for part in range(parts):
        chosen = pl.ds(part * rows, rows)
        mixed[chosen] = (1.0 - MIX_RATE) * sigma_ref[chosen] + new_ref[chosen]
        copy = pltpu.make_async_copy(mixed.at[chosen], out_hbm.at[chosen], done.at[part])
        copy.start()
        copies.append(copy)
    for copy in copies:
        copy.wait()


def fused_body(sigma_in, hamiltonian, coupling, energies, counts, strengths, offsets):
    points, order = sigma_in.shape[0], sigma_in.shape[3]
    ranks = lax.axis_size("energy")
    moments = lax.axis_size("mom")
    tiles = 2 * order // SUBLANES
    held = tiles // (ranks * moments)
    total = ranks * points
    span = total * SUBLANES
    cuts = 2 if order % 256 == 0 else 1
    hbm = pl.BlockSpec(memory_space=pltpu.HBM)
    operands = (energies, counts, strengths, offsets, sigma_in[:, 0], hamiltonian[0], coupling[0])
    sigma_new, sigma_held = pl.pallas_call(
        functools.partial(kernel, ranks, moments, points, order, held),
        out_shape=[
            jax.ShapeDtypeStruct((points, tiles, SUBLANES, order), jnp.float32),
            jax.ShapeDtypeStruct((points, 2, order, order), jnp.float32),
        ],
        in_specs=[hbm] * 7,
        out_specs=[pl.BlockSpec(memory_space=pltpu.VMEM)] * 2,
        scratch_shapes=[
            pltpu.VMEM((points, tiles, SUBLANES, order), jnp.float32),
            pltpu.VMEM((moments, held, total, SUBLANES, order), jnp.float32),
            pltpu.VMEM((moments, held, total, SUBLANES, order), jnp.float32),
            pltpu.VMEM((span, span), jnp.float32),
            pltpu.VMEM((2, order, order), jnp.bfloat16),
            pltpu.VMEM((2, order, order), jnp.bfloat16),
            pltpu.VMEM((2, order, order), jnp.float32),
            pltpu.VMEM((order, order), jnp.float32),
            pltpu.SMEM(energies.shape, jnp.float32),
            pltpu.SMEM(counts.shape, jnp.int32),
            pltpu.SMEM(strengths.shape, jnp.float32),
            pltpu.SMEM(offsets.shape, jnp.int32),
            pltpu.SemaphoreType.REGULAR,
            pltpu.SemaphoreType.DMA((points, 2)),
            pltpu.SemaphoreType.DMA((7,)),
            pltpu.SemaphoreType.DMA,
            pltpu.SemaphoreType.DMA((held + held // 2 * cuts,)),
            pltpu.SemaphoreType.DMA,
            pltpu.SemaphoreType.DMA,
        ],
        compiler_params=pltpu.CompilerParams(
            collective_id=0, has_side_effects=True, vmem_limit_bytes=32 * 1024 * 1024,
        ),
        name="green_and_scatter",
    )(*[pltpu.with_memory_space_constraint(value, pltpu.HBM) for value in operands])
    cells = (points * tiles, SUBLANES, order)
    vmem = pl.BlockSpec(memory_space=pltpu.VMEM)
    parts = 4
    result = pl.pallas_call(
        functools.partial(finish, parts),
        out_shape=jax.ShapeDtypeStruct(cells, jnp.float32),
        in_specs=[vmem] * 2,
        out_specs=pl.BlockSpec(memory_space=pltpu.HBM),
        scratch_shapes=[pltpu.VMEM(cells, jnp.float32), pltpu.SemaphoreType.DMA((parts,))],
        compiler_params=pltpu.CompilerParams(vmem_limit_bytes=8 * 1024 * 1024),
        name="mix",
    )(sigma_held.reshape(cells), sigma_new.reshape(cells))
    return result.reshape(sigma_in.shape)


def body(sigma_in, hamiltonian, coupling, energies, counts, strengths, offsets):
    devices = lax.axis_size("energy") * lax.axis_size("mom")
    tiles = 2 * sigma_in.shape[3] // SUBLANES
    fits = tiles % (2 * devices) == 0 and lax.axis_size("energy") % 8 == 0 and sigma_in.shape[0] > 1
    chosen = fused_body if fits else plain_body
    return chosen(sigma_in, hamiltonian, coupling, energies, counts, strengths, offsets)


def solution(mesh):
    placed = (
        P("energy", "mom", None, None, None),
        P("mom", None, None, None),
        P("mom", None, None),
        P(),
        P(),
        P(),
        P(),
    )
    return jax.shard_map(
        body,
        mesh=mesh,
        in_specs=placed,
        out_specs=P("energy", "mom", None, None, None),
        check_vma=False,
    )
```

```python
import functools

import jax
import jax.numpy as jnp
from jax import lax
from jax.experimental import pallas as pl
from jax.experimental.pallas import tpu as pltpu
from jax.sharding import PartitionSpec as P

PRECISE = lax.Precision.HIGHEST
MIX_RATE = 0.6
PHONON = 0.1
BROADENING = 0.02


def shifted(value, axis, steps):
    count = lax.axis_size(axis)
    pairs = [(source, (source + steps) % count) for source in range(count)]
    return lax.ppermute(value, axis, pairs)


def product(left_side, right_side):
    return jnp.dot(left_side, right_side, precision=PRECISE, preferred_element_type=jnp.float32)


def invert(matrix, energy, sweeps):
    identity = jnp.eye(matrix.shape[0], dtype=jnp.float32)

    def keep_going(carried):
        return carried[0] < sweeps

    def sweep(carried):
        estimate = carried[1]
        return (carried[0] + 1, 2.0 * estimate - product(estimate, product(matrix, estimate)))

    return lax.while_loop(keep_going, sweep, (jnp.int32(0), identity / energy))[1]


def solve_point(ham_block, coupling_block, sigma_pair, energy, sweeps):
    identity = jnp.eye(ham_block.shape[1], dtype=jnp.float32)
    left_matrix = energy * identity - ham_block[0] - sigma_pair[0]
    left_inverse = invert(left_matrix, energy, sweeps)
    inverse_coupled = product(left_inverse, coupling_block)
    coupled_inverse = product(coupling_block.T, left_inverse)
    right_matrix = (
        energy * identity
        - ham_block[1]
        - sigma_pair[1]
        - product(coupling_block.T, inverse_coupled)
    )
    right_green = invert(right_matrix, energy, sweeps)
    left_green = left_inverse + product(product(inverse_coupled, right_green), coupled_inverse)
    return jnp.stack([left_green, right_green])


def lorentz(offset):
    scaled = offset / BROADENING
    return 1.0 / (1.0 + scaled * scaled)


def build_kernel(row_energy, column_energy):
    spacing = row_energy[:, None] - column_energy[None, :]
    kernel = lorentz(spacing - PHONON) + lorentz(spacing + PHONON)
    return kernel / jnp.sum(kernel, axis=1, keepdims=True)


def plain_body(sigma_in, hamiltonian, coupling, energies, counts, strengths, offsets):
    points = sigma_in.shape[0]
    order = sigma_in.shape[3]
    ranks = lax.axis_size("energy")
    moments = lax.axis_size("mom")
    my_rank = lax.axis_index("energy")
    own_energy = lax.dynamic_slice_in_dim(energies, my_rank * points, points)
    own_count = lax.dynamic_slice_in_dim(counts, my_rank * points, points)
    blocks = sigma_in[:, 0]

    def solve_held(held_point):
        return solve_point(hamiltonian[0], coupling[0], held_point[0], held_point[1], held_point[2])

    green_blocks = lax.map(solve_held, (blocks, own_energy, own_count))
    shift_index = jnp.arange(moments, dtype=jnp.int32)
    weights = jnp.sum(
        strengths[:, None] * (offsets[:, None] == shift_index[None, :]).astype(jnp.float32), axis=0
    )
    kernel = build_kernel(energies, energies)
    piece_width = 2 * order * order // ranks
    spread = green_blocks.reshape(points, ranks, moments, piece_width // moments)
    column = lax.all_to_all(spread, "energy", split_axis=1, concat_axis=0, tiled=True)[:, 0]
    rows_all = column.shape[0]
    flat_column = column.reshape(rows_all, -1)
    mixed_sum = weights[0] * flat_column
    for offset_step in range(1, moments):
        mixed_sum = mixed_sum + weights[offset_step] * shifted(flat_column, "mom", offset_step)
    sigma_part = product(kernel, mixed_sum).reshape(column.shape)
    result = lax.all_to_all(sigma_part[:, None], "energy", split_axis=0, concat_axis=1, tiled=True)
    sigma_new = result.reshape(sigma_in.shape)
    return (1.0 - MIX_RATE) * sigma_in + MIX_RATE * sigma_new


SUBLANES = 8
MESH_ID = pl.DeviceIdType.MESH


def split(value):
    high = value.astype(jnp.bfloat16)
    return high, (value - high.astype(jnp.float32)).astype(jnp.bfloat16)


left_parts = right_parts = split


def multiply(left_side, right_side):
    (high, low), (near, far) = left_side, right_side
    rows = high.shape[0] // 2
    both = [
        jnp.dot(jnp.concatenate([low[n * rows:(n + 1) * rows], high[n * rows:(n + 1) * rows]], axis=0), near, preferred_element_type=jnp.float32)
        for n in range(2)
    ]
    last = [jnp.dot(high[n * rows:(n + 1) * rows], far, preferred_element_type=jnp.float32) for n in range(2)]
    return jnp.concatenate([b[:rows] + l + b[rows:] for b, l in zip(both, last)], axis=0)


def series(ratio, energy, count, identity):
    square = multiply(left_parts(ratio), right_parts(ratio))
    total = identity + ratio
    right = right_parts(square)
    fourth = multiply(left_parts(square), right)
    short = total + multiply(left_parts(total), right)
    right = right_parts(fourth)
    eighth = multiply(left_parts(fourth), right)
    total = short + multiply(left_parts(short), right)
    total = total + multiply(left_parts(total), right_parts(eighth))
    return jnp.where(count > 2, total, short) * (1.0 / energy)


def powers(ratio, identity, prepare):
    square = multiply(left_parts(ratio), right_parts(ratio))
    count = prepare()
    total = identity + ratio
    right = right_parts(square)
    fourth = multiply(left_parts(square), right)
    short = total + multiply(left_parts(total), right)
    fourth = jnp.where(count > 2, fourth, 0.0)
    right = right_parts(fourth)
    eighth = multiply(left_parts(fourth), right)
    total = short + multiply(left_parts(short), right)
    return total, eighth, count


def kernel(
    ranks, moments, points, order, held,
    energy_hbm, count_hbm, strength_hbm, offset_hbm, sigma_hbm, ham_hbm, coupling_hbm,
    out_ref, sigma_ref,
    green, gathered, mixed_out, wide, across, across_t,
    ham_ref, coupling_ref, energy_ref, count_ref, strength_ref, offset_ref,
    ready, read_sigma, read_other, send_first, recv_first, send_second, recv_second,
):
    devices = ranks * moments
    side = devices // 2
    group = side // 2
    total = ranks * points
    early = held // 2
    cuts = 2 if order % 256 == 0 else 1
    width = order // cuts
    my_rank = lax.axis_index("energy")
    my_moment = lax.axis_index("mom")
    me = my_rank * moments + my_moment
    my_side = me // side
    spot = lax.rem(me, side)
    near_side = my_side * side
    far_side = (1 - my_side) * side

    def place_of(other):
        return {"energy": other // moments, "mom": lax.rem(other, moments)}

    sources = [
        (coupling_hbm, coupling_ref), (ham_hbm.at[0], ham_ref.at[0]), (ham_hbm.at[1], ham_ref.at[1]),
        (energy_hbm, energy_ref), (count_hbm, count_ref), (strength_hbm, strength_ref), (offset_hbm, offset_ref),
    ]
    reads = [pltpu.make_async_copy(a, b, read_other.at[n]) for n, (a, b) in enumerate(sources)]

    def sigma_read(point, slab):
        return pltpu.make_async_copy(
            sigma_hbm.at[point, slab], sigma_ref.at[point, slab], read_sigma.at[point, slab]
        )

    for read in [reads[3], reads[1], sigma_read(0, 0), reads[4]]:
        read.start()
    barrier = pltpu.get_barrier_semaphore()

    quarter = ranks // 4
    blocks = quarter // 2
    my_block = lax.rem(lax.div(my_rank, 2), blocks)
    my_core = lax.rem(my_rank, 2)

    def send_over(send, begin=0, end=side):
        def over(index, carried):
            turn = lax.div(index, group)
            layer = turn * my_side + (1 - turn) * (1 - my_side)
            step = group - 1 - lax.rem(index, group)
            block = lax.rem(my_block + lax.div(step, 2 * moments), blocks)
            moment = lax.rem(my_moment + lax.rem(lax.div(step, 2), moments), moments)
            core = lax.rem(my_core + lax.rem(step, 2), 2)
            rank = (1 - my_side) * (ranks // 2) + layer * quarter + block * 2 + core
            send(rank * moments + moment)
            return carried

        lax.fori_loop(begin, end, over, 0)

    def greet(other):
        pl.semaphore_signal(barrier, inc=1, device_id=place_of(other), device_id_type=MESH_ID)

    send_over(greet)
    for read in [reads[0], reads[2], sigma_read(0, 1)]:
        read.start()

    row_index = lax.broadcasted_iota(jnp.int32, (order, order), 0)
    identity = (row_index == lax.broadcasted_iota(jnp.int32, (order, order), 1)).astype(jnp.float32)

    def tile_of(other, piece):
        return (held - 1 - piece) * devices + other

    def send_within(send):
        def within(index, carried):
            send(near_side + lax.rem(spot + index, side))
            return carried

        lax.fori_loop(1, side, within, 0)

    def first_of(piece, semaphore, point=None, cut=None):
        if cut is None:
            landing = gathered.at[my_moment, piece, my_rank * points + point]
            source_of = lambda other: green.at[point, tile_of(other, piece)]
        else:
            later, chosen = pl.ds(1, points - 1), pl.ds(cut * width, width)
            landing = gathered.at[my_moment, piece, pl.ds(my_rank * points + 1, points - 1), :, chosen]
            source_of = lambda other: green.at[later, tile_of(other, piece), :, chosen]

        def send(other):
            pltpu.make_async_remote_copy(
                src_ref=source_of(other), dst_ref=landing,
                send_sem=send_first, recv_sem=recv_first.at[semaphore],
                device_id=place_of(other), device_id_type=MESH_ID,
            ).start()

        def keep():
            pltpu.make_async_copy(source_of(me), landing, recv_first.at[semaphore]).start()

        return send, keep

    for read in [reads[3], reads[1], sigma_read(0, 0)]:
        read.wait()
    tiles = order // SUBLANES

    def solve(point, first):
        if not first:
            sigma_read(point, 0).wait()
            sigma_read(point, 1).wait()
        energy = energy_ref[my_rank * points + point]
        ratio = (ham_ref[0] + sigma_ref[point, 0]) * (1.0 / energy)

        def prepare():
            if first:
                reads[0].wait()
                reads[4].wait()
                across[0], across[1] = split(coupling_ref[...])
                across_t[0], across_t[1] = split(coupling_ref[...].T)
            return count_ref[my_rank * points + point]

        total, last, count = powers(ratio, identity, prepare)
        spread = coupling_ref[...] + multiply(left_parts(last), (across[0], across[1]))
        back = multiply((across_t[0], across_t[1]), right_parts(total))

        fold = multiply(left_parts(back), right_parts(spread)) * (1.0 / energy)
        if first:
            reads[2].wait()
            sigma_read(0, 1).wait()
        ratio = (ham_ref[1] + sigma_ref[point, 1] + fold) * (1.0 / energy)
        right_green = series(ratio, energy, count, identity)
        green[point, tiles:] = right_green.reshape(tiles, SUBLANES, order)

        if first:
            pl.semaphore_wait(barrier, side)
            mirror = lax.rem(me + side, devices)
            pl.semaphore_signal(ready, inc=1, device_id=place_of(mirror), device_id_type=MESH_ID)

        for piece in range(early):
            send_over(first_of(piece, piece, point=point)[0])
        if first:
            for read in reads[5:]:
                read.start()

            def read_point(point, carried):
                sigma_read(point, 0).start()
                sigma_read(point, 1).start()
                return carried

            lax.fori_loop(1, points, read_point, 0)
        else:

            @pl.when(point == 1)
            def _():
                pl.semaphore_wait(ready, 1)
                for piece in range(held):
                    send, keep = first_of(piece, piece, point=0)
                    keep()
                    send_within(send)

        right = right_parts(last)
        left_inverse = (total + multiply(left_parts(total), right)) * (1.0 / energy)
        back = (back + multiply(left_parts(back), right)) * (1.0 / energy)
        coupled = multiply(left_parts(total), right_parts(spread)) * (1.0 / energy)
        inner = multiply(left_parts(coupled), right_parts(right_green))
        left_green = left_inverse + multiply(left_parts(inner), right_parts(back))
        green[point, :tiles] = left_green.reshape(tiles, SUBLANES, order)

        if first:
            for piece in range(early, held):
                send_over(first_of(piece, piece, point=0)[0])
        else:
            for piece in range(early):
                send, keep = first_of(piece, piece, point=point)
                keep()
                send_within(send)

    def solve_later(point, carried):
        solve(point, False)
        return carried

    solve(0, True)
    lax.fori_loop(1, points, solve_later, 0)

    for piece in range(early, held):
        for cut in range(cuts):
            send, keep = first_of(piece, held + (piece - early) * cuts + cut, cut=cut)
            keep()
            send_over(send)
            send_within(send)

    for read in reads[5:]:
        read.wait()
    span = total * SUBLANES
    column = lax.broadcasted_iota(jnp.int32, (SUBLANES, span), 1)
    lane_slot = lax.rem(column, SUBLANES)
    lane_point = lax.div(column, SUBLANES)
    same = lane_slot == lax.broadcasted_iota(jnp.int32, (SUBLANES, span), 0)

    def place(index, carried):
        return jnp.where(lane_point == index, energy_ref[index], carried)

    column_energy = lax.fori_loop(0, total, place, jnp.zeros((SUBLANES, span), jnp.float32))

    def build(index, carried):
        spacing = energy_ref[index] - column_energy
        row = lorentz(spacing - PHONON) + lorentz(spacing + PHONON)
        row = jnp.where(same, row, 0.0)
        row = row * (MIX_RATE / jnp.sum(row, axis=1, keepdims=True))
        wide[pl.ds(pl.multiple_of(index * SUBLANES, SUBLANES), SUBLANES), :] = row
        return carried

    lax.fori_loop(0, total, build, 0)
    weights = []
    for step in range(moments):
        weight = jnp.float32(0.0)
        for transfer in range(strength_ref.shape[0]):
            weight = weight + jnp.where(offset_ref[transfer] == step, strength_ref[transfer], 0.0)
        weights.append(weight)

    wide_parts = left_parts(wide[...])
    arrivals = [(piece, None) for piece in range(early)] + [
        (piece, cut) for piece in range(early, held) for cut in range(cuts)
    ]

    waiting = []

    def settle(landed, semaphore):
        pltpu.make_async_copy(landed, landed, recv_first.at[semaphore]).wait()

    for piece, cut in arrivals:
        if cut is None:
            chosen = slice(None)
            settle(gathered.at[:, piece], piece)
        else:
            chosen = slice(cut * width, (cut + 1) * width)
            if cut == 0:
                settle(gathered.at[:, piece, pl.ds(0, ranks)], piece)
            settle(
                gathered.at[:, piece, pl.ds(0, total - ranks), :, chosen],
                held + (piece - early) * cuts + cut,
            )
        for moment in range(moments):
            scattered = weights[0] * gathered[moment, piece, :, :, chosen]
            for step in range(1, moments):
                source = (moment - step) % moments
                scattered = scattered + weights[step] * gathered[source, piece, :, :, chosen]
            columns = scattered.shape[-1]
            result = multiply(wide_parts, right_parts(scattered.reshape(span, columns)))
            mixed_out[moment, piece, :, :, chosen] = result.reshape(total, SUBLANES, columns)

        def give_back(other, piece=piece, chosen=chosen):
            rank = other // moments
            pltpu.make_async_remote_copy(
                src_ref=mixed_out.at[lax.rem(other, moments), piece, pl.ds(rank * points, points), :, chosen],
                dst_ref=out_ref.at[:, tile_of(me, piece), :, chosen],
                send_sem=send_second,
                recv_sem=recv_second,
                device_id=place_of(other),
                device_id_type=MESH_ID,
            ).start()

        held_back = piece == held - 1 and cuts > 1
        if held_back:
            send_over(give_back, 0, group)
        else:
            send_over(give_back)
        send_within(give_back)
        if held_back:
            waiting.append(give_back)
        pltpu.make_async_copy(
            mixed_out.at[my_moment, piece, pl.ds(my_rank * points, points), :, chosen],
            out_ref.at[:, tile_of(me, piece), :, chosen],
            recv_second,
        ).start()

    for give_back in waiting:
        send_over(give_back, group, side)

    pltpu.make_async_copy(out_ref, out_ref, recv_second).wait()
    sent = green.at[:, pl.ds(0, (devices - 1) * held)]
    pltpu.make_async_copy(sent, sent, send_first).wait()
    pltpu.make_async_copy(sent, sent, send_second).wait()


def finish(parts, sigma_ref, new_ref, out_hbm, mixed, done):
    rows = sigma_ref.shape[0] // parts
    copies = []
    for part in range(parts):
        chosen = pl.ds(part * rows, rows)
        mixed[chosen] = (1.0 - MIX_RATE) * sigma_ref[chosen] + new_ref[chosen]
        copy = pltpu.make_async_copy(mixed.at[chosen], out_hbm.at[chosen], done.at[part])
        copy.start()
        copies.append(copy)
    for copy in copies:
        copy.wait()


def fused_body(sigma_in, hamiltonian, coupling, energies, counts, strengths, offsets):
    points, order = sigma_in.shape[0], sigma_in.shape[3]
    ranks = lax.axis_size("energy")
    moments = lax.axis_size("mom")
    tiles = 2 * order // SUBLANES
    held = tiles // (ranks * moments)
    total = ranks * points
    span = total * SUBLANES
    cuts = 2 if order % 256 == 0 else 1
    hbm = pl.BlockSpec(memory_space=pltpu.HBM)
    operands = (energies, counts, strengths, offsets, sigma_in[:, 0], hamiltonian[0], coupling[0])
    sigma_new, sigma_held = pl.pallas_call(
        functools.partial(kernel, ranks, moments, points, order, held),
        out_shape=[
            jax.ShapeDtypeStruct((points, tiles, SUBLANES, order), jnp.float32),
            jax.ShapeDtypeStruct((points, 2, order, order), jnp.float32),
        ],
        in_specs=[hbm] * 7,
        out_specs=[pl.BlockSpec(memory_space=pltpu.VMEM)] * 2,
        scratch_shapes=[
            pltpu.VMEM((points, tiles, SUBLANES, order), jnp.float32),
            pltpu.VMEM((moments, held, total, SUBLANES, order), jnp.float32),
            pltpu.VMEM((moments, held, total, SUBLANES, order), jnp.float32),
            pltpu.VMEM((span, span), jnp.float32),
            pltpu.VMEM((2, order, order), jnp.bfloat16),
            pltpu.VMEM((2, order, order), jnp.bfloat16),
            pltpu.VMEM((2, order, order), jnp.float32),
            pltpu.VMEM((order, order), jnp.float32),
            pltpu.SMEM(energies.shape, jnp.float32),
            pltpu.SMEM(counts.shape, jnp.int32),
            pltpu.SMEM(strengths.shape, jnp.float32),
            pltpu.SMEM(offsets.shape, jnp.int32),
            pltpu.SemaphoreType.REGULAR,
            pltpu.SemaphoreType.DMA((points, 2)),
            pltpu.SemaphoreType.DMA((7,)),
            pltpu.SemaphoreType.DMA,
            pltpu.SemaphoreType.DMA((held + held // 2 * cuts,)),
            pltpu.SemaphoreType.DMA,
            pltpu.SemaphoreType.DMA,
        ],
        compiler_params=pltpu.CompilerParams(
            collective_id=0, has_side_effects=True, vmem_limit_bytes=32 * 1024 * 1024,
        ),
        name="green_and_scatter",
    )(*[pltpu.with_memory_space_constraint(value, pltpu.HBM) for value in operands])
    cells = (points * tiles, SUBLANES, order)
    vmem = pl.BlockSpec(memory_space=pltpu.VMEM)
    parts = 4
    result = pl.pallas_call(
        functools.partial(finish, parts),
        out_shape=jax.ShapeDtypeStruct(cells, jnp.float32),
        in_specs=[vmem] * 2,
        out_specs=pl.BlockSpec(memory_space=pltpu.HBM),
        scratch_shapes=[pltpu.VMEM(cells, jnp.float32), pltpu.SemaphoreType.DMA((parts,))],
        compiler_params=pltpu.CompilerParams(vmem_limit_bytes=8 * 1024 * 1024),
        name="mix",
    )(sigma_held.reshape(cells), sigma_new.reshape(cells))
    return result.reshape(sigma_in.shape)


def body(sigma_in, hamiltonian, coupling, energies, counts, strengths, offsets):
    devices = lax.axis_size("energy") * lax.axis_size("mom")
    tiles = 2 * sigma_in.shape[3] // SUBLANES
    fits = tiles % (2 * devices) == 0 and lax.axis_size("energy") % 8 == 0 and sigma_in.shape[0] > 1
    chosen = fused_body if fits else plain_body
    return chosen(sigma_in, hamiltonian, coupling, energies, counts, strengths, offsets)


def solution(mesh):
    placed = (
        P("energy", "mom", None, None, None),
        P("mom", None, None, None),
        P("mom", None, None),
        P(),
        P(),
        P(),
        P(),
    )
    return jax.shard_map(
        body,
        mesh=mesh,
        in_specs=placed,
        out_specs=P("energy", "mom", None, None, None),
        check_vma=False,
    )
```
